128 devices in a mesh: ta: 2 (over x_hi), ha: 16 (over z, x_lo, core), wa: 4 (over y).
Axes of the slice: x: 4 (x_hi: 2, x_lo: 2; x = x_hi * 2 + x_lo), y: 4, z: 4, core: 2. Of those that a mesh axis runs over, the one named last changes fastest.
Arguments:
- features: bfloat16 [8, 512, 128, 128], P('ta', 'ha', 'wa'), may hold values from -6 to 6
- kernel_one: bfloat16 [3, 3, 3, 128, 128], replicated, may hold values from -0.109375 to 0.109375
- kernel_two: bfloat16 [3, 3, 3, 128, 128], replicated, may hold values from -0.109375 to 0.109375
Outputs:
- decoded: bfloat16 [8, 512, 128, 128], P('ta', 'ha', 'wa')
The draws below stay inside these ranges and needn't reach their ends.
All inputs are finite; a program needn't handle non-finite values.
Results may differ from the reference program's by a relative error of at most 0.0075.
Values may be sent and summed in bfloat16 or wider, within the bound.
A program may use at most 64 MiB of HBM per device.

```python
import jax
import jax.numpy as jnp
from jax import lax

C = 128
FRAMES = 8
HEIGHT = 512
WIDTH = 128


def block_scale(rng, dims, split, low, top_value):
    factor_of, own = 1.0, jax.random.fold_in(rng, 6)
    for position, shards_of in split:
        heights = jnp.exp(jax.random.uniform(jax.random.fold_in(own, position), (shards_of,), jnp.float32, low / len(split), top_value / len(split)))
        factor_of = factor_of * jnp.repeat(heights, dims[position] // shards_of).reshape([-1 if axis == position else 1 for axis in range(len(dims))])
    return factor_of


def scatter_about(stream_key, shape, scale, reach, cuts=(), kind=jnp.bfloat16):
    values = jax.random.normal(stream_key, shape, jnp.float32) * scale
    if len(cuts) > 0:
        values = block_scale(stream_key, shape, cuts, -0.22, 0.18) * values
    return jnp.clip(values, min=-reach, max=reach).astype(kind)


def setup_inputs(seed: int = 0) -> dict:
    key_of = jax.random.split(jax.random.key(seed), 4)
    return {
        "features": scatter_about(key_of[0], (FRAMES, HEIGHT, WIDTH, C), 1.0, 6.0, ((0, 2), (1, 16), (2, 4))),
        "kernel_one": scatter_about(key_of[1], (3, 3, 3, C, C), (27 * C) ** -0.5, 0.109375),
        "kernel_two": scatter_about(key_of[2], (3, 3, 3, C, C), (27 * C) ** -0.5, 0.109375),
    }


def normed_silu(values):
    values = values.astype(jnp.float32)
    scaled = values * lax.rsqrt(lax.optimization_barrier(jnp.mean(values * values, axis=-1, keepdims=True)) + 1e-06)
    return jax.nn.silu(scaled).astype(jnp.bfloat16)

def convolve(volume, kernel):
    result = lax.conv_general_dilated(volume.astype(jnp.float32)[None], kernel.astype(jnp.float32), (1, 1, 1), 'SAME', dimension_numbers=('NDHWC', 'DHWIO', 'NDHWC'), precision=lax.Precision.HIGHEST)
    return result[0]

def reference(features, kernel_one, kernel_two):
    act_one = normed_silu(features)
    hidden = convolve(act_one, kernel_one).astype(jnp.bfloat16)
    act_two = normed_silu(hidden)
    summed = features.astype(jnp.float32) + convolve(act_two, kernel_two)
    return summed.astype(jnp.bfloat16)
```

```python
import jax
import jax.numpy as jnp
from jax import lax
from jax.experimental import pallas as pl
from jax.experimental.pallas import tpu as pltpu
from jax.sharding import PartitionSpec as P

MESH = pl.DeviceIdType.MESH
F32, BF16 = jnp.float32, jnp.bfloat16
T, H, W, C = 4, 32, 32, 128
R = 16
DIRS = [(dh, dw) for dh in (-1, 0, 1) for dw in (-1, 0, 1) if (dh, dw) != (0, 0)]


def normed_silu(v):
    u = v * lax.rsqrt(jnp.mean(v * v, axis=-1, keepdims=True) + 1e-06)
    half = 0.5 * u
    return half * (1.0 + jnp.tanh(half))


def kernel(x_hbm, k1_hbm, k2_hbm, o_ref, xv, face, halo, s1, s2, t1, t2, acc,
           cs1, cr1, cs2, cr2, send, recv, local):
    ta, ha, wa = (lax.axis_index(a) for a in ("ta", "ha", "wa"))
    nh, nw = lax.axis_size("ha"), lax.axis_size("wa")
    has_h = {-1: ha > 0, 0: True, 1: ha < nh - 1}
    has_w = {-1: wa > 0, 0: True, 1: wa < nw - 1}

    def frame(g):
        return g + ta * (3 - 2 * g)

    def exists(d):
        return jnp.logical_and(has_h[d[0]], has_w[d[1]])

    def device(d, flip):
        return {"ta": 1 - ta if flip else ta, "ha": ha + d[0], "wa": wa + d[1]}

    def remote(src, dst, s, r, dev):
        return pltpu.make_async_remote_copy(
            src_ref=src, dst_ref=dst, send_sem=send.at[s], recv_sem=recv.at[r],
            device_id=dev, device_id_type=MESH)

    side = {-1: 0, 1: 1}

    def rim(d, group):
        dh, dw = d
        base, flip = 8 * group, group in (1, 4)
        i, j = DIRS.index(d), DIRS.index((-dh, -dw))
        if group in (0, 1):
            here, there = (pl.ds(0, T), pl.ds(0, T)) if group == 0 else (3, 4)
            cs, cr = cs1, cr1
        elif group == 4:
            here, there, cs, cr = 3, 4, cs2, cr2
        else:
            here = there = pl.ds(2 * (group - 2), 2)
            cs, cr = cs2, cr2
        row = 0 if dh < 0 else H - 1
        slot = 33 if dh < 0 else 0
        if dw == 0:
            if group == 0:
                src, dst = x_hbm.at[:, row], halo.at[side[-dh], pl.ds(0, T)]
            elif group == 1:
                src, dst = x_hbm.at[frame(3), row], halo.at[side[-dh], 4]
            else:
                src = s2.at[here, row + 1, :, pl.ds(128, 128)]
                dst = s2.at[there, slot, :, pl.ds(128, 128)]
        elif dh == 0:
            src = cs.at[side[dw], here]
            dst = cr.at[side[-dw], there, pl.ds(1, H)]
        else:
            src = cs.at[side[dw], here, row]
            dst = cr.at[side[-dw], there, slot]
        return remote(src, dst, base + i, base + j, device(d, flip))

    def each(dirs, group, act):
        for d in dirs:
            @pl.when(exists(d))
            def _():
                act(rim(d, group))

    def start_rims(dirs, group):
        each(dirs, group, lambda c: c.start())

    def wait_rims(dirs, group):
        for d in dirs:
            @pl.when(exists(d))
            def _():
                rim((-d[0], -d[1]), group).wait_recv()

    rows_only = [d for d in DIRS if d[1] == 0]
    columns = [d for d in DIRS if d[1] != 0]

    here = {"ta": 1 - ta, "ha": ha, "wa": wa}
    cuts = [(0, R + 1), (R + 1, H - R - 1)]

    def face_copy(i):
        a, n = cuts[i]
        return remote(x_hbm.at[frame(3), pl.ds(a, n)], face.at[pl.ds(a, n)], 40 + i, 40 + i, here)

    def face2_copy(i):
        rows = pl.ds(1 + R * i, R)
        return remote(s2.at[3, rows, :, pl.ds(128, 128)], s2.at[4, rows, :, pl.ds(128, 128)],
                      42 + i, 42 + i, here)

    loads = [pltpu.make_async_copy(x_hbm.at[g], xv.at[g], local.at[g]) for g in range(T)]
    for c in loads:
        c.start()
    weights = []
    for n, (k, t) in enumerate(((k1_hbm, t1), (k2_hbm, t2))):
        for i in range(3):
            tap = 1 + (i - 1) * (1 - 2 * ta)
            for part in range(2):
                weights.append(pltpu.make_async_copy(
                    k.at[tap], t.at[i + part, :, :, pl.ds(128 * part, 128)],
                    local.at[T + 6 * n + 2 * i + part]))
    for c in weights:
        c.start()

    for cr in (cr1, cr2):
        cr[...] = jnp.zeros_like(cr)
    halo[...] = jnp.zeros_like(halo)
    for r in (0, H + 1):
        s2[:, r] = jnp.zeros((T + 1, W, 3 * C), BF16)

    barrier = pltpu.get_barrier_semaphore()
    for d in DIRS:
        for flip in (False, True):
            @pl.when(exists(d))
            def _():
                pl.semaphore_signal(barrier, inc=1, device_id=device(d, flip), device_id_type=MESH)
    pl.semaphore_signal(barrier, inc=1, device_id=here, device_id_type=MESH)
    count_h = 1 + (ha > 0).astype(jnp.int32) + (ha < nh - 1).astype(jnp.int32)
    count_w = 1 + (wa > 0).astype(jnp.int32) + (wa < nw - 1).astype(jnp.int32)
    pl.semaphore_wait(barrier, 2 * count_h * count_w - 1)

    start_rims(rows_only, 0)
    start_rims(rows_only, 1)
    for i in range(2):
        face_copy(i).start()

    def shifted(s, g, rows, a):
        column = lax.broadcasted_iota(jnp.int32, a.shape, 1)
        s[g, rows, :, 0:C] = jnp.where(column == 0, 0.0, pltpu.roll(a, 1, 1)).astype(BF16)
        s[g, rows, :, 2 * C:] = jnp.where(column == W - 1, 0.0, pltpu.roll(a, W - 1, 1)).astype(BF16)

    def spread(s, g, r0, n, a):
        rows = pl.ds(r0, n)
        s[g, rows, :, C:2 * C] = a.astype(BF16)
        shifted(s, g, rows, a)

    def edges(cs, g, r0, n, a):
        cs[0, g, pl.ds(r0, n)] = a[:, 0:1, :]
        cs[1, g, pl.ds(r0, n)] = a[:, W - 1:W, :]

    def insert(s, cr, g):
        def step(i, _):
            rows = pl.ds(17 * i, 17)
            line = lax.broadcasted_iota(jnp.int32, (17, 16, C), 1)
            left = s[g, rows, 0:16, 0:C].astype(F32)
            s[g, rows, 0:16, 0:C] = jnp.where(line == 0, cr[0, g, rows], left).astype(BF16)
            right = s[g, rows, 16:32, 2 * C:].astype(F32)
            s[g, rows, 16:32, 2 * C:] = jnp.where(line == 15, cr[1, g, rows], right).astype(BF16)
            return 0
        lax.fori_loop(0, 2, step, 0)

    def halo_rows(g, at):
        for k, r in ((0, 0), (1, H + 1)):
            spread(s1, g, r, 1, normed_silu(halo[k, at].astype(F32))[None])

    def halo_rows2(g):
        for r in (0, H + 1):
            rows = pl.ds(r, 1)
            shifted(s2, g, rows, s2[g, rows, :, C:2 * C].astype(F32))

    def conv(s, t, first, j0, h0):
        parts = [s[first + j - j0, pl.ds(h0 + kh, R)].reshape(R * W, 3 * C)
                 for j in range(j0, 4) for kh in range(3)]
        taps = t[j0:4].reshape((4 - j0) * 9 * C, 2 * C)
        acc[...] = jnp.dot(jnp.concatenate(parts, axis=1), taps, preferred_element_type=F32)

    def activate(g0, h0):
        def step(i, _):
            for e in range(2):
                hid = acc[pl.ds(pl.multiple_of(i * 8 * W, 8 * W), 8 * W), e * C:(e + 1) * C]
                a = normed_silu(hid.astype(BF16).astype(F32)).reshape(8, W, C)
                spread(s2, g0 + e, 1 + h0 + 8 * i, 8, a)
                edges(cs2, g0 + e, h0 + 8 * i, 8, a)
            return 0
        lax.fori_loop(0, R // 8, step, 0)

    def finish(g0, h0):
        def step(i, _):
            for e in range(2):
                f = frame(g0 + e)
                out = acc[pl.ds(pl.multiple_of(i * 8 * W, 8 * W), 8 * W), e * C:(e + 1) * C]
                rows = pl.ds(h0 + 8 * i, 8)
                x = xv[f, rows].astype(F32)
                o_ref[f, rows] = (x + out.reshape(8, W, C)).astype(BF16)
            return 0
        lax.fori_loop(0, R // 8, step, 0)

    for c in loads:
        c.wait()

    def first_act(i, _):
        g, h0 = i // 4, (i % 4) * 8
        a = normed_silu(xv[frame(g), pl.ds(h0, 8)].astype(F32))
        spread(s1, g, 1 + h0, 8, a)
        edges(cs1, g, h0, 8, a)
        return 0
    lax.fori_loop(0, 4 * T, first_act, 0)
    start_rims(columns, 0)
    start_rims(columns, 1)

    for t in (t1, t2):
        t[0, :, :, C:] = jnp.zeros((9, C, C), BF16)
        t[3, :, :, 0:C] = jnp.zeros((9, C, C), BF16)

    wait_rims(rows_only, 0)
    for g in range(T):
        halo_rows(g, frame(g))
    wait_rims(columns, 0)
    for g in range(T):
        insert(s1, cr1, g)
    for c in weights[:6]:
        c.wait()

    def pair_a(i, _):
        conv(s1, t1, 0, 1, i * R)
        activate(0, i * R)
        return 0
    lax.fori_loop(0, H // R, pair_a, 0)
    start_rims(DIRS, 2)

    wait_rims(rows_only, 1)
    halo_rows(4, 4)
    wait_rims(columns, 1)
    for i in range(2):
        face_copy(i).wait_recv()
        a, n = cuts[i]
        for r in range(a, a + n, 8):
            m = min(8, a + n - r)
            spread(s1, 4, 1 + r, m, normed_silu(face[pl.ds(r, m)].astype(F32)))
        insert(s1, cr1, 4)
        conv(s1, t1, 1, 0, i * R)
        activate(2, i * R)
        face2_copy(i).start()
    start_rims(DIRS, 4)
    start_rims(DIRS, 3)

    for c in weights[6:]:
        c.wait()
    wait_rims(DIRS, 2)
    wait_rims(DIRS, 3)
    for g in range(T):
        halo_rows2(g)
        insert(s2, cr2, g)

    def pair_b(i, _):
        conv(s2, t2, 0, 1, i * R)
        finish(0, i * R)
        return 0
    lax.fori_loop(0, H // R, pair_b, 0)

    wait_rims(DIRS, 4)
    halo_rows2(4)
    for i in range(2):
        face2_copy(i).wait_recv()
    for r in range(0, H, 8):
        rows = pl.ds(1 + r, 8)
        shifted(s2, 4, rows, s2[4, rows, :, C:2 * C].astype(F32))
    insert(s2, cr2, 4)

    def pair_c(i, _):
        conv(s2, t2, 1, 0, i * R)
        finish(2, i * R)
        return 0
    lax.fori_loop(0, H // R, pair_c, 0)

    for group in range(5):
        each(DIRS, group, lambda c: c.wait_send())
    for i in range(2):
        face_copy(i).wait_send()
        face2_copy(i).wait_send()


def body(features, kernel_one, kernel_two):
    return pl.pallas_call(
        kernel,
        out_shape=jax.ShapeDtypeStruct((T, H, W, C), BF16),
        in_specs=[pl.BlockSpec(memory_space=pl.ANY)] * 3,
        out_specs=pl.BlockSpec(memory_space=pltpu.VMEM),
        scratch_shapes=[
            pltpu.VMEM((T, H, W, C), BF16),
            pltpu.VMEM((H, W, C), BF16),
            pltpu.VMEM((2, T + 1, W, C), BF16),
            pltpu.VMEM((T + 1, H + 2, W, 3 * C), BF16),
            pltpu.VMEM((T + 1, H + 2, W, 3 * C), BF16),
            pltpu.VMEM((4, 9, C, 2 * C), BF16),
            pltpu.VMEM((4, 9, C, 2 * C), BF16),
            pltpu.VMEM((R * W, 2 * C), F32),
            pltpu.VMEM((2, T, H, 1, C), F32),
            pltpu.VMEM((2, T + 1, H + 2, 1, C), F32),
            pltpu.VMEM((2, T, H, 1, C), F32),
            pltpu.VMEM((2, T + 1, H + 2, 1, C), F32),
            pltpu.SemaphoreType.DMA((44,)),
            pltpu.SemaphoreType.DMA((44,)),
            pltpu.SemaphoreType.DMA((T + 12,)),
        ],
        compiler_params=pltpu.CompilerParams(
            collective_id=0, has_side_effects=True, vmem_limit_bytes=60 << 20),
        name="resblock",
    )(features, kernel_one.reshape(3, 9, C, C), kernel_two.reshape(3, 9, C, C))


def solution(mesh):
    return jax.shard_map(
        body,
        mesh=mesh,
        in_specs=(P("ta", "ha", "wa", None), P(), P()),
        out_specs=P("ta", "ha", "wa", None),
        check_vma=False,
    )
```

```python
import jax
import jax.numpy as jnp
from jax import lax
from jax.experimental import pallas as pl
from jax.experimental.pallas import tpu as pltpu
from jax.sharding import PartitionSpec as P

MESH = pl.DeviceIdType.MESH
F32, BF16 = jnp.float32, jnp.bfloat16
T, H, W, C = 4, 32, 32, 128
R = 16
DIRS = [(dh, dw) for dh in (-1, 0, 1) for dw in (-1, 0, 1) if (dh, dw) != (0, 0)]
ROWS = [d for d in DIRS if d[1] == 0]
COLUMNS = [d for d in DIRS if d[1] != 0]
LEFT, MID, RIGHT = slice(0, C), slice(C, 2 * C), slice(2 * C, 3 * C)
EARLY, LATE, BOTH = slice(0, C), slice(C, 2 * C), slice(0, 2 * C)


def normed_silu(v):
    half = v * lax.rsqrt(jnp.sum(v * v, axis=-1, keepdims=True) * (4.0 / C) + 4e-06)
    return half + half * jnp.tanh(half)


def kernel(x_hbm, k1_hbm, k2_hbm, o_ref, xv, face, halo, s1, s2, t1, t2, acc, pair,
           cs1, cr1, cs2, cr2, bytes_of, send, recv, local):
    ta, ha, wa = (lax.axis_index(a) for a in ("ta", "ha", "wa"))
    nh, nw = lax.axis_size("ha"), lax.axis_size("wa")

    def frame(g):
        return g + ta * (3 - 2 * g)

    def device(d, flip):
        return {"ta": 1 - ta if flip else ta, "ha": lax.rem(ha + d[0] + nh, nh),
                "wa": lax.rem(wa + d[1] + nw, nw)}

    def remote(src, dst, r, dev):
        return pltpu.make_async_remote_copy(
            src_ref=src, dst_ref=dst, send_sem=send.at[r], recv_sem=recv.at[r],
            device_id=dev, device_id_type=MESH)

    side = {-1: 0, 1: 1}

    groups = {
        "raw": (x_hbm, None, pl.ds(0, T), T, False),
        "raw_cut": (x_hbm, None, T, 1, True),
        "one_123": (s1, pl.ds(1, 3), pl.ds(1, 3), 3, False),
        "one_0": (s1, 0, 0, 1, False),
        "one_cut": (s1, 3, T, 1, True),
        "two_2": (s2, 2, 2, 1, False),
        "two_3": (s2, 3, 3, 1, False),
        "two_cut": (s2, 3, T, 1, True),
        "two_01": (s2, pl.ds(0, 2), pl.ds(0, 2), 2, False),
    }
    names = list(groups)

    def dirs_of(group):
        return ROWS if "raw" in group else COLUMNS if "one" in group else DIRS

    def start_rims(group):
        source, mine, theirs, _, flip = groups[group]
        cs, cr = (cs2, cr2) if source is s2 else (cs1, cr1)
        for dh, dw in dirs_of(group):
            row = 0 if dh < 0 else H - 1
            slot = H + 1 if dh < 0 else 0
            if dw == 0 and source is x_hbm:
                src = x_hbm.at[frame(3), row] if flip else x_hbm.at[:, row]
                dst = halo.at[side[-dh], theirs]
            elif dw == 0:
                src = s2.at[mine, row + 1, :, pl.ds(C, C)]
                dst = s2.at[theirs, slot, :, pl.ds(C, C)]
            elif dh == 0:
                src = cs.at[side[dw], mine]
                dst = cr.at[side[-dw], theirs, pl.ds(1, H)]
            else:
                src = cs.at[side[dw], mine, row]
                dst = cr.at[side[-dw], theirs, slot]
            remote(src, dst, names.index(group), device((dh, dw), flip)).start()

    def lines(group):
        n = groups[group][3]
        rows, columns = 2 * n * W // 2, 2 * n * (H + 2)
        return rows if "raw" in group else columns if "one" in group else rows + columns

    def wait_lines(sem, n):
        pltpu.make_async_copy(bytes_of.at[pl.ds(0, n)], bytes_of.at[pl.ds(0, n)], sem).wait()

    def wait_rims(group):
        wait_lines(recv.at[names.index(group)], lines(group))

    partner = {"ta": 1 - ta, "ha": ha, "wa": wa}
    cuts = [(0, R + 1), (R + 1, H - R - 1)]

    def face_copy(i):
        a, n = cuts[i]
        return remote(x_hbm.at[frame(3), pl.ds(a, n)], face.at[pl.ds(a, n)], 9 + i, partner)

    def face2_copy(i):
        rows = pl.ds(1 + R * i, R)
        return remote(s2.at[3, rows, :, pl.ds(C, C)], s2.at[T, rows, :, pl.ds(C, C)], 11 + i, partner)

    loads = [pltpu.make_async_copy(x_hbm.at[frame(g)], xv.at[frame(g)], local.at[g])
             for g in range(T)]
    for c in loads[::-1]:
        c.start()
    weights = []
    for n, (k, t) in enumerate(((k1_hbm, t1), (k2_hbm, t2))):
        for i in range(3):
            tap = 1 + (i - 1) * (1 - 2 * ta)
            for part in range(2):
                weights.append(pltpu.make_async_copy(
                    k.at[tap], t.at[i + part, :, :, pl.ds(C * part, C)],
                    local.at[T + 6 * n + 2 * i + part]))
    for c in weights[:6]:
        c.start()

    barrier = pltpu.get_barrier_semaphore()
    for d in DIRS:
        for flip in (False, True):
            pl.semaphore_signal(barrier, inc=1, device_id=device(d, flip), device_id_type=MESH)
    pl.semaphore_signal(barrier, inc=1, device_id=partner, device_id_type=MESH)
    for t in (t1, t2):
        t[0, :, :, LATE] = jnp.zeros((9, C, C), BF16)
        t[3, :, :, EARLY] = jnp.zeros((9, C, C), BF16)
    pl.semaphore_wait(barrier, 2 * len(DIRS) + 1)

    start_rims("raw")
    start_rims("raw_cut")
    for i in range(2):
        face_copy(i).start()

    inside = ((0, ha > 0), (H + 1, ha < nh - 1))
    first_column = jnp.where(wa > 0, 0, -1)
    last_column = jnp.where(wa < nw - 1, 15, -1)

    def spread(s, g, r0, n, a):
        rows = pl.ds(r0, n)
        column = lax.broadcasted_iota(jnp.int32, a.shape, 1)
        s[g, rows, :, MID] = a.astype(BF16)
        s[g, rows, :, LEFT] = jnp.where(column == 0, 0.0, pltpu.roll(a, 1, 1)).astype(BF16)
        s[g, rows, :, RIGHT] = jnp.where(column == W - 1, 0.0, pltpu.roll(a, W - 1, 1)).astype(BF16)

    def edges(cs, g, r0, n, a):
        cs[0, g, pl.ds(r0, n)] = a[:, 0:1, :]
        cs[1, g, pl.ds(r0, n)] = a[:, W - 1:W, :]

    def rim_rows(s, cr, g):
        for r, there in inside:
            rows = pl.ds(r, 1)
            a = s[g, rows, :, MID].astype(F32)
            column = lax.broadcasted_iota(jnp.int32, a.shape, 1)
            left = jnp.where(column == 0, jnp.where(wa > 0, cr[0, g, rows], 0.0), pltpu.roll(a, 1, 1))
            right = jnp.where(column == W - 1, jnp.where(wa < nw - 1, cr[1, g, rows], 0.0),
                              pltpu.roll(a, W - 1, 1))
            for lanes, v in ((LEFT, left), (MID, a), (RIGHT, right)):
                s[g, rows, :, lanes] = jnp.where(there, v, 0.0).astype(BF16)

    def insert(s, cr, g):
        def step(i, _):
            rows = pl.ds(1 + 16 * i, 16)
            line = lax.broadcasted_iota(jnp.int32, (16, 16, C), 1)
            left = s[g, rows, 0:16, LEFT].astype(F32)
            s[g, rows, 0:16, LEFT] = jnp.where(line == first_column, cr[0, g, rows], left).astype(BF16)
            right = s[g, rows, 16:32, RIGHT].astype(F32)
            s[g, rows, 16:32, RIGHT] = jnp.where(line == last_column, cr[1, g, rows], right).astype(BF16)
            return 0
        lax.fori_loop(0, 2, step, 0)

    def dot(s, t, pairs, h0, columns=(0, 1, 2), lanes=BOTH):
        parts, taps = [], []
        for f, j in pairs:
            for kh in range(3):
                rows = pl.ds(h0 + kh, R)
                for kw in columns:
                    parts.append(s[f, rows, :, kw * C:(kw + 1) * C].reshape(R * W, C))
                    taps.append(t[j, 3 * kh + kw, :, lanes])
        return jnp.dot(jnp.concatenate(parts, axis=1), jnp.concatenate(taps, axis=0),
                       preferred_element_type=F32)

    def rows_of(h0, n=R):
        return pl.ds(h0 * W if isinstance(h0, int) else pl.multiple_of(h0 * W, n * W), n * W)

    def activate(sums, lanes, g, h0):
        def step(i, _):
            r = h0 + 8 * i
            hid = sums[rows_of(r, 8), lanes]
            a = normed_silu(hid.astype(BF16).astype(F32)).reshape(8, W, C)
            spread(s2, g, 1 + r, 8, a)
            edges(cs2, g, r, 8, a)
            return 0
        lax.fori_loop(0, R // 8, step, 0)

    def finish(out, g, h0):
        rows = pl.ds(h0, R)
        o_ref[frame(g), rows] = (xv[frame(g), rows].astype(F32) + out.reshape(R, W, C)).astype(BF16)

    def blocks(step):
        lax.fori_loop(0, H // R, lambda i, _: step(i * R) or 0, 0)

    def first_act(g):
        loads[g].wait()
        def step(i, _):
            a = normed_silu(xv[frame(g), pl.ds(8 * i, 8)].astype(F32))
            spread(s1, g, 1 + 8 * i, 8, a)
            edges(cs1, g, 8 * i, 8, a)
            return 0
        lax.fori_loop(0, H // 8, step, 0)

    for g in (3, 2, 1):
        first_act(g)
    start_rims("one_123")
    start_rims("one_cut")
    first_act(0)
    start_rims("one_0")
    for c in weights[6:]:
        c.start()

    def halo_rows(g, at):
        for k in range(2):
            a = jnp.where(inside[k][1], normed_silu(halo[k, at].astype(F32)), 0.0)
            s1[g, inside[k][0], :, MID] = a.astype(BF16)

    wait_rims("raw")
    for g in range(T):
        halo_rows(g, frame(g))
    for c in weights[:6]:
        c.wait()

    def middle(h0):
        acc[rows_of(h0), :] = dot(s1, t1, ((1, 0), (2, 1), (3, 2)), h0, (1,))
        pair[rows_of(h0), :] = dot(s1, t1, ((0, 1), (1, 2), (2, 3)), h0, (1,))
    blocks(middle)
    wait_rims("one_123")
    for g in (1, 2, 3):
        rim_rows(s1, cr1, g)
        insert(s1, cr1, g)

    def inner(h0):
        acc[rows_of(h0), :] += dot(s1, t1, ((1, 0), (2, 1), (3, 2)), h0, (0, 2))
        activate(acc, EARLY, 2, h0)
    blocks(inner)
    start_rims("two_2")
    wait_rims("one_0")
    rim_rows(s1, cr1, 0)
    insert(s1, cr1, 0)
    wait_rims("raw_cut")
    halo_rows(T, T)
    wait_rims("one_cut")
    rim_rows(s1, cr1, T)

    for i in range(2):
        h0 = i * R
        face_copy(i).wait_recv()
        a, n = cuts[i]
        def face_act(k, _):
            r = a + 8 * k
            spread(s1, T, 1 + r, 8, normed_silu(face[pl.ds(r, 8)].astype(F32)))
            return 0
        whole = n // 8
        lax.fori_loop(0, whole, face_act, 0)
        if n % 8:
            r = a + 8 * whole
            spread(s1, T, 1 + r, n % 8, normed_silu(face[pl.ds(r, n % 8)].astype(F32)))
        insert(s1, cr1, T)
        acc[rows_of(h0), LATE] += dot(s1, t1, ((T, 3),), h0, lanes=LATE)
        activate(acc, LATE, 3, h0)
        face2_copy(i).start()
        if i == 1:
            start_rims("two_cut")
            start_rims("two_3")
        pair[rows_of(h0), :] += dot(s1, t1, ((0, 1), (1, 2), (2, 3)), h0, (0, 2))
        activate(pair, EARLY, 0, h0)
        activate(pair, LATE, 1, h0)
    start_rims("two_01")

    def rims_in(group, frames):
        wait_rims(group)
        for g in frames:
            rim_rows(s2, cr2, g)
            insert(s2, cr2, g)

    for c in weights[6:]:
        c.wait()
    rims_in("two_2", (2,))
    def two(h0):
        acc[rows_of(h0), :] = dot(s2, t2, ((2, 1),), h0)
        pair[rows_of(h0), LATE] = dot(s2, t2, ((2, 3),), h0, lanes=LATE)
    blocks(two)
    rims_in("two_3", (3,))
    def three(h0):
        acc[rows_of(h0), :] += dot(s2, t2, ((3, 2),), h0)
    blocks(three)
    rims_in("two_01", (0, 1))

    def outer(h0):
        d = dot(s2, t2, ((0, 1), (1, 2)), h0)
        finish(d[:, EARLY], 0, h0)
        finish(d[:, LATE] + pair[rows_of(h0), LATE], 1, h0)
    blocks(outer)

    def one(h0):
        finish(acc[rows_of(h0), EARLY] + dot(s2, t2, ((1, 0),), h0, lanes=EARLY), 2, h0)
    blocks(one)

    wait_rims("two_cut")
    for i in range(2):
        face2_copy(i).wait_recv()
    def face_shift(k, _):
        rows = pl.ds(1 + 8 * k, 8)
        a = s2[T, rows, :, MID].astype(F32)
        column = lax.broadcasted_iota(jnp.int32, a.shape, 1)
        s2[T, rows, :, LEFT] = jnp.where(column == 0, 0.0, pltpu.roll(a, 1, 1)).astype(BF16)
        s2[T, rows, :, RIGHT] = jnp.where(column == W - 1, 0.0, pltpu.roll(a, W - 1, 1)).astype(BF16)
        return 0
    lax.fori_loop(0, H // 8, face_shift, 0)
    rim_rows(s2, cr2, T)
    insert(s2, cr2, T)

    def last(h0):
        finish(acc[rows_of(h0), LATE] + dot(s2, t2, ((T, 3),), h0, lanes=LATE), 3, h0)
    blocks(last)

    for group in groups:
        wait_lines(send.at[names.index(group)], lines(group))
    for i in range(2):
        face_copy(i).wait_send()
        face2_copy(i).wait_send()


def body(features, kernel_one, kernel_two):
    return pl.pallas_call(
        kernel,
        out_shape=jax.ShapeDtypeStruct((T, H, W, C), BF16),
        in_specs=[pl.BlockSpec(memory_space=pl.ANY)] * 3,
        out_specs=pl.BlockSpec(memory_space=pltpu.VMEM),
        scratch_shapes=[
            pltpu.VMEM((T, H, W, C), BF16),
            pltpu.VMEM((H, W, C), BF16),
            pltpu.VMEM((2, T + 1, W, C), BF16),
            pltpu.VMEM((T + 1, H + 2, W, 3 * C), BF16),
            pltpu.VMEM((T + 1, H + 2, W, 3 * C), BF16),
            pltpu.VMEM((4, 9, C, 2 * C), BF16),
            pltpu.VMEM((4, 9, C, 2 * C), BF16),
            pltpu.VMEM((H * W, 2 * C), F32),
            pltpu.VMEM((H * W, 2 * C), F32),
            pltpu.VMEM((2, T, H, 1, C), F32),
            pltpu.VMEM((2, T + 1, H + 2, 1, C), F32),
            pltpu.VMEM((2, T, H, 1, C), F32),
            pltpu.VMEM((2, T + 1, H + 2, 1, C), F32),
            pltpu.VMEM((256, 1, C), F32),
            pltpu.SemaphoreType.DMA((13,)),
            pltpu.SemaphoreType.DMA((13,)),
            pltpu.SemaphoreType.DMA((T + 12,)),
        ],
        compiler_params=pltpu.CompilerParams(
            collective_id=0, has_side_effects=True, vmem_limit_bytes=60 << 20),
        name="resblock",
    )(features, kernel_one.reshape(3, 9, C, C), kernel_two.reshape(3, 9, C, C))


def solution(mesh):
    return jax.shard_map(
        body,
        mesh=mesh,
        in_specs=(P("ta", "ha", "wa", None), P(), P()),
        out_specs=P("ta", "ha", "wa", None),
        check_vma=False,
    )
```

```python
import jax
import jax.numpy as jnp
from jax import lax
from jax.experimental import pallas as pl
from jax.experimental.pallas import tpu as pltpu
from jax.sharding import PartitionSpec as P

MESH = pl.DeviceIdType.MESH
F32, BF16 = jnp.float32, jnp.bfloat16
T, H, W, C = 4, 32, 32, 128
R = 16
DIRS = [(dh, dw) for dh in (-1, 0, 1) for dw in (-1, 0, 1) if (dh, dw) != (0, 0)]
ROWS = [d for d in DIRS if d[1] == 0]
COLUMNS = [d for d in DIRS if d[1] != 0]
LEFT, MID, RIGHT = slice(0, C), slice(C, 2 * C), slice(2 * C, 3 * C)
EARLY, LATE, BOTH = slice(0, C), slice(C, 2 * C), slice(0, 2 * C)


def normed_silu(v):
    half = v * lax.rsqrt(jnp.sum(v * v, axis=-1, keepdims=True) * (4.0 / C) + 4e-06)
    return half + half * jnp.tanh(half)


def kernel(x_hbm, k1_hbm, k2_hbm, o_ref, xv, face, halo, s1, s2, t1, t2, acc, pair,
           cs1, cr1, cs2, cr2, bytes_of, send, recv, local):
    ta, ha, wa = (lax.axis_index(a) for a in ("ta", "ha", "wa"))
    nh, nw = lax.axis_size("ha"), lax.axis_size("wa")

    def frame(g):
        return g + ta * (3 - 2 * g)

    def device(d, flip):
        return {"ta": 1 - ta if flip else ta, "ha": lax.rem(ha + d[0] + nh, nh),
                "wa": lax.rem(wa + d[1] + nw, nw)}

    def remote(src, dst, r, dev):
        return pltpu.make_async_remote_copy(
            src_ref=src, dst_ref=dst, send_sem=send.at[r], recv_sem=recv.at[r],
            device_id=dev, device_id_type=MESH)

    side = {-1: 0, 1: 1}

    groups = {
        "raw": (x_hbm, None, pl.ds(0, T), T, False),
        "raw_cut": (x_hbm, None, T, 1, True),
        "one": (s1, pl.ds(0, T), pl.ds(0, T), T, False),
        "one_cut": (s1, 3, T, 1, True),
        "two_2": (s2, 2, 2, 1, False),
        "two_3": (s2, 3, 3, 1, False),
        "two_cut": (s2, 3, T, 1, True),
        "two_01": (s2, pl.ds(0, 2), pl.ds(0, 2), 2, False),
    }
    names = list(groups)

    def dirs_of(group):
        return ROWS if "raw" in group else COLUMNS if "one" in group else DIRS

    def start_rims(group):
        source, mine, theirs, _, flip = groups[group]
        cs, cr = (cs2, cr2) if source is s2 else (cs1, cr1)
        for dh, dw in dirs_of(group):
            row = 0 if dh < 0 else H - 1
            slot = H + 1 if dh < 0 else 0
            if dw == 0 and source is x_hbm:
                src = x_hbm.at[frame(3), row] if flip else x_hbm.at[:, row]
                dst = halo.at[side[-dh], theirs]
            elif dw == 0:
                src = s2.at[mine, row + 1, :, pl.ds(C, C)]
                dst = s2.at[theirs, slot, :, pl.ds(C, C)]
            elif dh == 0:
                src = cs.at[side[dw], mine]
                dst = cr.at[side[-dw], theirs, pl.ds(1, H)]
            else:
                src = cs.at[side[dw], mine, row]
                dst = cr.at[side[-dw], theirs, slot]
            remote(src, dst, names.index(group), device((dh, dw), flip)).start()

    def lines(group):
        n = groups[group][3]
        rows, columns = 2 * n * W // 2, 2 * n * (H + 2)
        return rows if "raw" in group else columns if "one" in group else rows + columns

    def wait_lines(sem, n):
        pltpu.make_async_copy(bytes_of.at[pl.ds(0, n)], bytes_of.at[pl.ds(0, n)], sem).wait()

    def wait_rims(group):
        wait_lines(recv.at[names.index(group)], lines(group))

    partner = {"ta": 1 - ta, "ha": ha, "wa": wa}
    cuts = [(0, 8), (8, R - 7), (R + 1, H - R - 1)]
    cuts2 = [(0, R), (R, 8), (R + 8, 8)]

    def face_copy(i):
        a, n = cuts[i]
        return remote(x_hbm.at[frame(3), pl.ds(a, n)], face.at[pl.ds(a, n)], 8 + i, partner)

    def face2_copy(i):
        rows = pl.ds(1 + cuts2[i][0], cuts2[i][1])
        return remote(s2.at[3, rows, :, pl.ds(C, C)], s2.at[T, rows, :, pl.ds(C, C)], 11 + i, partner)

    loads = [pltpu.make_async_copy(x_hbm.at[frame(g)], xv.at[frame(g)], local.at[g])
             for g in range(T)]
    for c in loads[::-1]:
        c.start()
    weights = []
    for n, (k, t) in enumerate(((k1_hbm, t1), (k2_hbm, t2))):
        for i in range(3):
            tap = 1 + (i - 1) * (1 - 2 * ta)
            for part in range(2):
                weights.append(pltpu.make_async_copy(
                    k.at[tap], t.at[i + part, :, :, pl.ds(C * part, C)],
                    local.at[T + 6 * n + 2 * i + part]))
    for c in weights[:6]:
        c.start()

    barrier = pltpu.get_barrier_semaphore()
    for d in DIRS:
        for flip in (False, True):
            pl.semaphore_signal(barrier, inc=1, device_id=device(d, flip), device_id_type=MESH)
    pl.semaphore_signal(barrier, inc=1, device_id=partner, device_id_type=MESH)
    for t in (t1, t2):
        t[0, :, :, LATE] = jnp.zeros((9, C, C), BF16)
        t[3, :, :, EARLY] = jnp.zeros((9, C, C), BF16)
    pl.semaphore_wait(barrier, 2 * len(DIRS) + 1)

    start_rims("raw")
    start_rims("raw_cut")
    face_copy(0).start()

    inside = ((0, ha > 0), (H + 1, ha < nh - 1))
    first_column = jnp.where(wa > 0, 0, -1)
    last_column = jnp.where(wa < nw - 1, 15, -1)

    def spread(s, g, r0, n, a):
        rows = pl.ds(r0, n)
        column = lax.broadcasted_iota(jnp.int32, a.shape, 1)
        s[g, rows, :, MID] = a.astype(BF16)
        s[g, rows, :, LEFT] = jnp.where(column == 0, 0.0, pltpu.roll(a, 1, 1)).astype(BF16)
        s[g, rows, :, RIGHT] = jnp.where(column == W - 1, 0.0, pltpu.roll(a, W - 1, 1)).astype(BF16)

    def edges(cs, g, r0, n, a):
        cs[0, g, pl.ds(r0, n)] = a[:, 0:1, :]
        cs[1, g, pl.ds(r0, n)] = a[:, W - 1:W, :]

    def rim_rows(s, cr, g):
        for r, there in inside:
            rows = pl.ds(r, 1)
            a = s[g, rows, :, MID].astype(F32)
            column = lax.broadcasted_iota(jnp.int32, a.shape, 1)
            left = jnp.where(column == 0, jnp.where(wa > 0, cr[0, g, rows], 0.0), pltpu.roll(a, 1, 1))
            right = jnp.where(column == W - 1, jnp.where(wa < nw - 1, cr[1, g, rows], 0.0),
                              pltpu.roll(a, W - 1, 1))
            for lanes, v in ((LEFT, left), (MID, a), (RIGHT, right)):
                s[g, rows, :, lanes] = jnp.where(there, v, 0.0).astype(BF16)

    def insert(s, cr, g):
        def step(i, _):
            rows = pl.ds(1 + 16 * i, 16)
            line = lax.broadcasted_iota(jnp.int32, (16, 16, C), 1)
            left = s[g, rows, 0:16, LEFT].astype(F32)
            s[g, rows, 0:16, LEFT] = jnp.where(line == first_column, cr[0, g, rows], left).astype(BF16)
            right = s[g, rows, 16:32, RIGHT].astype(F32)
            s[g, rows, 16:32, RIGHT] = jnp.where(line == last_column, cr[1, g, rows], right).astype(BF16)
            return 0
        lax.fori_loop(0, 2, step, 0)

    def dot(s, t, pairs, h0, columns=(0, 1, 2), lanes=BOTH):
        parts, taps = [], []
        for f, j in pairs:
            for kh in range(3):
                rows = pl.ds(h0 + kh, R)
                for kw in columns:
                    parts.append(s[f, rows, :, kw * C:(kw + 1) * C].reshape(R * W, C))
                    taps.append(t[j, 3 * kh + kw, :, lanes])
        return jnp.dot(jnp.concatenate(parts, axis=1), jnp.concatenate(taps, axis=0),
                       preferred_element_type=F32)

    def rows_of(h0, n=R):
        return pl.ds(h0 * W if isinstance(h0, int) else pl.multiple_of(h0 * W, n * W), n * W)

    def activate(sums, lanes, g, h0):
        def step(i, _):
            r = h0 + 8 * i
            hid = sums[rows_of(r, 8), lanes]
            a = normed_silu(hid.astype(BF16).astype(F32)).reshape(8, W, C)
            spread(s2, g, 1 + r, 8, a)
            edges(cs2, g, r, 8, a)
            return 0
        lax.fori_loop(0, R // 8, step, 0)

    def finish(out, g, h0):
        rows = pl.ds(h0, R)
        o_ref[frame(g), rows] = (xv[frame(g), rows].astype(F32) + out.reshape(R, W, C)).astype(BF16)

    def blocks(step):
        lax.fori_loop(0, H // R, lambda i, _: step(i * R) or 0, 0)

    def outer_columns(g):
        loads[g].wait()
        def step(i, _):
            rows = pl.ds(8 * i, 8)
            for k in range(2):
                a = normed_silu(xv[frame(g), rows, 24 * k:24 * k + 8].astype(F32))
                cs1[k, g, rows] = a[:, 7 * k:7 * k + 1, :]
            return 0
        lax.fori_loop(0, H // 8, step, 0)

    for g in (3, 2, 1, 0):
        outer_columns(g)
    start_rims("one")
    start_rims("one_cut")
    for i in (1, 2):
        face_copy(i).start()
    for c in weights[6:]:
        c.start()

    def first_act(i, _):
        g, r = i // 4, 8 * (i % 4)
        spread(s1, g, 1 + r, 8, normed_silu(xv[frame(g), pl.ds(r, 8)].astype(F32)))
        return 0
    lax.fori_loop(0, 4 * T, first_act, 0)

    def halo_rows(g, at):
        for k in range(2):
            a = jnp.where(inside[k][1], normed_silu(halo[k, at].astype(F32)), 0.0)
            s1[g, inside[k][0], :, MID] = a.astype(BF16)

    wait_rims("raw")
    for g in range(T):
        halo_rows(g, frame(g))
    for c in weights[:6]:
        c.wait()

    def middle(h0):
        acc[rows_of(h0), :] = dot(s1, t1, ((1, 0), (2, 1), (3, 2)), h0, (1,))
        pair[rows_of(h0), :] = dot(s1, t1, ((0, 1), (1, 2), (2, 3)), h0, (1,))
    blocks(middle)
    wait_rims("one")
    for g in range(T):
        rim_rows(s1, cr1, g)
        insert(s1, cr1, g)

    def inner(h0):
        acc[rows_of(h0), :] += dot(s1, t1, ((1, 0), (2, 1), (3, 2)), h0, (0, 2))
        activate(acc, EARLY, 2, h0)
    blocks(inner)
    start_rims("two_2")
    wait_rims("raw_cut")
    halo_rows(T, T)
    wait_rims("one_cut")
    rim_rows(s1, cr1, T)

    for i in range(2):
        h0 = i * R
        for piece in ((0, 1), (2,))[i]:
            face_copy(piece).wait_recv()
        a, n = ((0, R + 1), (R + 1, H - R - 1))[i]
        def face_act(k, _):
            r = a + 8 * k
            spread(s1, T, 1 + r, 8, normed_silu(face[pl.ds(r, 8)].astype(F32)))
            return 0
        whole = n // 8
        lax.fori_loop(0, whole, face_act, 0)
        if n % 8:
            r = a + 8 * whole
            spread(s1, T, 1 + r, n % 8, normed_silu(face[pl.ds(r, n % 8)].astype(F32)))
        insert(s1, cr1, T)
        acc[rows_of(h0), LATE] += dot(s1, t1, ((T, 3),), h0, lanes=LATE)
        activate(acc, LATE, 3, h0)
        if i == 1:
            start_rims("two_3")
            start_rims("two_cut")
        face2_copy(i).start()
        pair[rows_of(h0), :] += dot(s1, t1, ((0, 1), (1, 2), (2, 3)), h0, (0, 2))
        activate(pair, EARLY, 0, h0)
        activate(pair, LATE, 1, h0)
    start_rims("two_01")
    face2_copy(2).start()

    def rims_in(group, frames):
        wait_rims(group)
        for g in frames:
            rim_rows(s2, cr2, g)
            insert(s2, cr2, g)

    for c in weights[6:]:
        c.wait()
    rims_in("two_2", (2,))
    def two(h0):
        acc[rows_of(h0), :] = dot(s2, t2, ((2, 1),), h0)
        pair[rows_of(h0), LATE] = dot(s2, t2, ((2, 3),), h0, lanes=LATE)
    blocks(two)
    rims_in("two_3", (3,))
    def three(h0):
        acc[rows_of(h0), :] += dot(s2, t2, ((3, 2),), h0)
    blocks(three)
    rims_in("two_01", (0, 1))

    def outer(h0):
        d = dot(s2, t2, ((0, 1), (1, 2)), h0)
        finish(d[:, EARLY], 0, h0)
        finish(d[:, LATE] + pair[rows_of(h0), LATE], 1, h0)
    blocks(outer)

    def one(h0):
        finish(acc[rows_of(h0), EARLY] + dot(s2, t2, ((1, 0),), h0, lanes=EARLY), 2, h0)
    blocks(one)

    wait_rims("two_cut")
    for i in range(3):
        face2_copy(i).wait_recv()
    def face_shift(k, _):
        rows = pl.ds(1 + 8 * k, 8)
        a = s2[T, rows, :, MID].astype(F32)
        column = lax.broadcasted_iota(jnp.int32, a.shape, 1)
        s2[T, rows, :, LEFT] = jnp.where(column == 0, 0.0, pltpu.roll(a, 1, 1)).astype(BF16)
        s2[T, rows, :, RIGHT] = jnp.where(column == W - 1, 0.0, pltpu.roll(a, W - 1, 1)).astype(BF16)
        return 0
    lax.fori_loop(0, H // 8, face_shift, 0)
    rim_rows(s2, cr2, T)
    insert(s2, cr2, T)

    def last(h0):
        finish(acc[rows_of(h0), LATE] + dot(s2, t2, ((T, 3),), h0, lanes=LATE), 3, h0)
    blocks(last)

    for group in groups:
        wait_lines(send.at[names.index(group)], lines(group))
    for i in range(3):
        face_copy(i).wait_send()
        face2_copy(i).wait_send()


def place(x_ref, o_ref, sem):
    c = pltpu.make_async_copy(x_ref, o_ref, sem.at[0])
    c.start()
    c.wait()


def body(features, kernel_one, kernel_two):
    out = pl.pallas_call(
        kernel,
        out_shape=jax.ShapeDtypeStruct((T, H, W, C), BF16),
        in_specs=[pl.BlockSpec(memory_space=pltpu.HBM)] * 3,
        out_specs=pl.BlockSpec(memory_space=pltpu.VMEM),
        scratch_shapes=[
            pltpu.VMEM((T, H, W, C), BF16),
            pltpu.VMEM((H, W, C), BF16),
            pltpu.VMEM((2, T + 1, W, C), BF16),
            pltpu.VMEM((T + 1, H + 2, W, 3 * C), BF16),
            pltpu.VMEM((T + 1, H + 2, W, 3 * C), BF16),
            pltpu.VMEM((4, 9, C, 2 * C), BF16),
            pltpu.VMEM((4, 9, C, 2 * C), BF16),
            pltpu.VMEM((H * W, 2 * C), F32),
            pltpu.VMEM((H * W, 2 * C), F32),
            pltpu.VMEM((2, T, H, 1, C), F32),
            pltpu.VMEM((2, T + 1, H + 2, 1, C), F32),
            pltpu.VMEM((2, T, H, 1, C), F32),
            pltpu.VMEM((2, T + 1, H + 2, 1, C), F32),
            pltpu.VMEM((288, 1, C), F32),
            pltpu.SemaphoreType.DMA((14,)),
            pltpu.SemaphoreType.DMA((14,)),
            pltpu.SemaphoreType.DMA((T + 12,)),
        ],
        compiler_params=pltpu.CompilerParams(
            collective_id=0, has_side_effects=True, vmem_limit_bytes=26 << 20),
        name="resblock",
    )(*(pltpu.with_memory_space_constraint(a, pltpu.HBM) for a in (
        features, kernel_one.reshape(3, 9, C, C), kernel_two.reshape(3, 9, C, C))))
    return pl.pallas_call(
        place, out_shape=jax.ShapeDtypeStruct((T, H, W, C), BF16),
        in_specs=[pl.BlockSpec(memory_space=pl.ANY)], out_specs=pl.BlockSpec(memory_space=pl.ANY),
        scratch_shapes=[pltpu.SemaphoreType.DMA((1,))],
        compiler_params=pltpu.CompilerParams(vmem_limit_bytes=1 << 20), name="place")(out)


def solution(mesh):
    return jax.shard_map(
        body,
        mesh=mesh,
        in_specs=(P("ta", "ha", "wa", None), P(), P()),
        out_specs=P("ta", "ha", "wa", None),
        check_vma=False,
    )
```

```python
import jax
import jax.numpy as jnp
from jax import lax
from jax.experimental import pallas as pl
from jax.experimental.pallas import tpu as pltpu
from jax.sharding import PartitionSpec as P

MESH = pl.DeviceIdType.MESH
F32, BF16 = jnp.float32, jnp.bfloat16
T, H, W, C = 4, 32, 32, 128
R = 16
DIRS = [(dh, dw) for dh in (-1, 0, 1) for dw in (-1, 0, 1) if (dh, dw) != (0, 0)]
ROWS = [d for d in DIRS if d[1] == 0]
COLUMNS = [d for d in DIRS if d[1] != 0]
LEFT, MID, RIGHT = slice(0, C), slice(C, 2 * C), slice(2 * C, 3 * C)
EARLY, LATE, BOTH = slice(0, C), slice(C, 2 * C), slice(0, 2 * C)


def normed_silu(v):
    half = v * lax.rsqrt(jnp.sum(v * v, axis=-1, keepdims=True) * (4.0 / C) + 4e-06)
    return half + half * jnp.tanh(half)


def kernel(x_hbm, k1_hbm, k2_hbm, o_ref, xv, face, halo, s1, s2, t1, t2, acc, pair,
           cs1, cr1, cs2, cr2, shift, bytes_of, send, recv, local):
    ta, ha, wa = (lax.axis_index(a) for a in ("ta", "ha", "wa"))
    nh, nw = lax.axis_size("ha"), lax.axis_size("wa")

    def frame(g):
        return g + ta * (3 - 2 * g)

    def device(d, flip):
        return {"ta": 1 - ta if flip else ta, "ha": lax.rem(ha + d[0] + nh, nh),
                "wa": lax.rem(wa + d[1] + nw, nw)}

    def remote(src, dst, r, dev):
        return pltpu.make_async_remote_copy(
            src_ref=src, dst_ref=dst, send_sem=send.at[r], recv_sem=recv.at[r],
            device_id=dev, device_id_type=MESH)

    side = {-1: 0, 1: 1}

    groups = {
        "raw": (x_hbm, None, pl.ds(0, T), T, False),
        "raw_cut": (x_hbm, None, T, 1, True),
        "one": (s1, pl.ds(0, T), pl.ds(0, T), T, False),
        "one_cut": (s1, 3, T, 1, True),
        "two_2": (s2, 2, 2, 1, False),
        "two_3": (s2, 3, 3, 1, False),
        "two_cut": (s2, 3, T, 1, True),
        "two_01": (s2, pl.ds(0, 2), pl.ds(0, 2), 2, False),
    }
    names = list(groups)

    def dirs_of(group):
        return ROWS if "raw" in group else COLUMNS if "one" in group else DIRS

    def start_rims(group):
        source, mine, theirs, _, flip = groups[group]
        cs, cr = (cs2, cr2) if source is s2 else (cs1, cr1)
        for dh, dw in dirs_of(group):
            row = 0 if dh < 0 else H - 1
            slot = H + 1 if dh < 0 else 0
            if dw == 0 and source is x_hbm:
                src = x_hbm.at[frame(3), row] if flip else x_hbm.at[:, row]
                dst = halo.at[side[-dh], theirs]
            elif dw == 0:
                src = s2.at[mine, row + 1, :, pl.ds(C, C)]
                dst = s2.at[theirs, slot, :, pl.ds(C, C)]
            elif dh == 0:
                src = cs.at[side[dw], mine]
                dst = cr.at[side[-dw], theirs, pl.ds(1, H)]
            else:
                src = cs.at[side[dw], mine, row]
                dst = cr.at[side[-dw], theirs, slot]
            remote(src, dst, names.index(group), device((dh, dw), flip)).start()

    def lines(group):
        n = groups[group][3]
        rows, columns = 2 * n * W // 2, 2 * n * (H + 2)
        return rows if "raw" in group else columns if "one" in group else rows + columns

    def wait_lines(sem, n):
        pltpu.make_async_copy(bytes_of.at[pl.ds(0, n)], bytes_of.at[pl.ds(0, n)], sem).wait()

    def wait_rims(group):
        wait_lines(recv.at[names.index(group)], lines(group))

    partner = {"ta": 1 - ta, "ha": ha, "wa": wa}
    cuts = [(0, 8), (8, R - 7), (R + 1, H - R - 1)]
    cuts2 = [(0, R), (R, 8), (R + 8, 8)]

    def face_copy(i):
        a, n = cuts[i]
        return remote(x_hbm.at[frame(3), pl.ds(a, n)], face.at[pl.ds(a, n)], 8 + i, partner)

    def face2_copy(i):
        rows = pl.ds(1 + cuts2[i][0], cuts2[i][1])
        return remote(s2.at[3, rows, :, pl.ds(C, C)], s2.at[T, rows, :, pl.ds(C, C)], 11 + i, partner)

    loads = [pltpu.make_async_copy(x_hbm.at[frame(g)], xv.at[frame(g)], local.at[g])
             for g in range(T)]
    for c in loads[::-1]:
        c.start()
    weights = []
    for n, (k, t) in enumerate(((k1_hbm, t1), (k2_hbm, t2))):
        for i in range(3):
            tap = 1 + (i - 1) * (1 - 2 * ta)
            for part in range(2):
                weights.append(pltpu.make_async_copy(
                    k.at[tap], t.at[i + part, :, :, pl.ds(C * part, C)],
                    local.at[T + 6 * n + 2 * i + part]))
    for c in weights[:6]:
        c.start()

    barrier = pltpu.get_barrier_semaphore()
    for d in DIRS:
        for flip in (False, True):
            pl.semaphore_signal(barrier, inc=1, device_id=device(d, flip), device_id_type=MESH)
    pl.semaphore_signal(barrier, inc=1, device_id=partner, device_id_type=MESH)
    for t in (t1, t2):
        t[0, :, :, LATE] = jnp.zeros((9, C, C), BF16)
        t[3, :, :, EARLY] = jnp.zeros((9, C, C), BF16)
    shift[:, 0:8] = jnp.zeros((R, 8, C), F32)
    shift[:, 8 + W:] = jnp.zeros((R, 8, C), F32)
    inside = ((0, ha > 0), (H + 1, ha < nh - 1))
    first_column = jnp.where(wa > 0, 0, -1)
    last_column = jnp.where(wa < nw - 1, 15, -1)

    before = 7 + lax.div(ta, 2)
    after = before + 2

    def shifted(s, g, r0, n, a):
        rows = pl.ds(r0, n)
        shift[0:n, 8:8 + W] = a
        s[g, rows, :, LEFT] = shift[0:n, pl.ds(before, W)].astype(BF16)
        s[g, rows, :, RIGHT] = shift[0:n, pl.ds(after, W)].astype(BF16)

    def spread(s, g, r0, n, a):
        s[g, pl.ds(r0, n), :, MID] = a.astype(BF16)
        shifted(s, g, r0, n, a)

    def edges(cs, g, r0, n, a):
        cs[0, g, pl.ds(r0, n)] = a[:, 0:1, :]
        cs[1, g, pl.ds(r0, n)] = a[:, W - 1:W, :]

    def rim_rows(s, cr, g):
        for r, there in inside:
            rows = pl.ds(r, 1)
            a = s[g, rows, :, MID].astype(F32)
            column = lax.broadcasted_iota(jnp.int32, a.shape, 1)
            left = jnp.where(column == 0, jnp.where(wa > 0, cr[0, g, rows], 0.0), pltpu.roll(a, 1, 1))
            right = jnp.where(column == W - 1, jnp.where(wa < nw - 1, cr[1, g, rows], 0.0),
                              pltpu.roll(a, W - 1, 1))
            for lanes, v in ((LEFT, left), (MID, a), (RIGHT, right)):
                s[g, rows, :, lanes] = jnp.where(there, v, 0.0).astype(BF16)

    def insert(s, cr, g):
        def step(i, _):
            rows = pl.ds(1 + 16 * i, 16)
            line = lax.broadcasted_iota(jnp.int32, (16, 16, C), 1)
            left = s[g, rows, 0:16, LEFT].astype(F32)
            s[g, rows, 0:16, LEFT] = jnp.where(line == first_column, cr[0, g, rows], left).astype(BF16)
            right = s[g, rows, 16:32, RIGHT].astype(F32)
            s[g, rows, 16:32, RIGHT] = jnp.where(line == last_column, cr[1, g, rows], right).astype(BF16)
            return 0
        lax.fori_loop(0, 2, step, 0)

    def dot(s, t, pairs, h0, columns=(0, 1, 2), lanes=BOTH):
        parts, taps = [], []
        for f, j in pairs:
            for kh in range(3):
                rows = pl.ds(h0 + kh, R)
                for kw in columns:
                    parts.append(s[f, rows, :, kw * C:(kw + 1) * C].reshape(R * W, C))
                    taps.append(t[j, 3 * kh + kw, :, lanes])
        return jnp.dot(jnp.concatenate(parts, axis=1), jnp.concatenate(taps, axis=0),
                       preferred_element_type=F32)

    def rows_of(h0, n=R):
        return pl.ds(h0 * W if isinstance(h0, int) else pl.multiple_of(h0 * W, n * W), n * W)

    def activate(sums, lanes, g, h0):
        def step(i, _):
            r = h0 + R * i
            hid = sums[rows_of(r, R), lanes]
            a = normed_silu(hid.astype(BF16).astype(F32)).reshape(R, W, C)
            spread(s2, g, 1 + r, R, a)
            edges(cs2, g, r, R, a)
            return 0
        lax.fori_loop(0, 1, step, 0)

    def finish(out, g, h0):
        rows = pl.ds(h0, R)
        o_ref[frame(g), rows] = (xv[frame(g), rows].astype(F32) + out.reshape(R, W, C)).astype(BF16)

    def blocks(step):
        lax.fori_loop(0, H // R, lambda i, _: step(i * R) or 0, 0)

    def outer_columns(g):
        loads[g].wait()
        for k in range(2):
            a = normed_silu(xv[frame(g), :, 24 * k:24 * k + 8].astype(F32))
            cs1[k, g] = a[:, 7 * k:7 * k + 1, :]

    for g in (3, 2, 1, 0):
        outer_columns(g)
    pl.semaphore_wait(barrier, 2 * len(DIRS) + 1)

    start_rims("raw")
    start_rims("raw_cut")
    start_rims("one")
    start_rims("one_cut")
    face_copy(0).start()
    for i in (1, 2):
        face_copy(i).start()
    for c in weights[6:]:
        c.start()

    def first_act(i, _):
        g, r = i // 2, R * (i % 2)
        spread(s1, g, 1 + r, R, normed_silu(xv[frame(g), pl.ds(r, R)].astype(F32)))
        return 0
    lax.fori_loop(0, 2 * T, first_act, 0)

    def halo_rows(g, at):
        for k in range(2):
            a = jnp.where(inside[k][1], normed_silu(halo[k, at].astype(F32)), 0.0)
            s1[g, inside[k][0], :, MID] = a.astype(BF16)

    wait_rims("raw")
    for g in range(T):
        halo_rows(g, frame(g))
    for c in weights[:6]:
        c.wait()

    def middle(h0):
        acc[rows_of(h0), :] = dot(s1, t1, ((1, 0), (2, 1), (3, 2)), h0, (1,))
        pair[rows_of(h0), :] = dot(s1, t1, ((0, 1), (1, 2), (2, 3)), h0, (1,))
    blocks(middle)
    wait_rims("one")
    for g in range(T):
        rim_rows(s1, cr1, g)
        insert(s1, cr1, g)

    def inner(h0):
        acc[rows_of(h0), :] += dot(s1, t1, ((1, 0), (2, 1), (3, 2)), h0, (0, 2))
        activate(acc, EARLY, 2, h0)
    blocks(inner)
    start_rims("two_2")
    wait_rims("raw_cut")
    halo_rows(T, T)
    wait_rims("one_cut")
    rim_rows(s1, cr1, T)

    for i in range(2):
        h0 = i * R
        for piece in ((0, 1), (2,))[i]:
            face_copy(piece).wait_recv()
        a, n = ((0, R + 1), (R + 1, H - R - 1))[i]
        def face_act(k, _):
            r = a + 8 * k
            spread(s1, T, 1 + r, 8, normed_silu(face[pl.ds(r, 8)].astype(F32)))
            return 0
        whole = n // 8
        lax.fori_loop(0, whole, face_act, 0)
        if n % 8:
            r = a + 8 * whole
            spread(s1, T, 1 + r, n % 8, normed_silu(face[pl.ds(r, n % 8)].astype(F32)))
        insert(s1, cr1, T)
        acc[rows_of(h0), LATE] += dot(s1, t1, ((T, 3),), h0, lanes=LATE)
        activate(acc, LATE, 3, h0)
        if i == 1:
            start_rims("two_3")
            start_rims("two_cut")
        face2_copy(i).start()
        pair[rows_of(h0), :] += dot(s1, t1, ((0, 1), (1, 2), (2, 3)), h0, (0, 2))
        activate(pair, EARLY, 0, h0)
        activate(pair, LATE, 1, h0)
    start_rims("two_01")
    face2_copy(2).start()

    def rims_in(group, frames):
        wait_rims(group)
        for g in frames:
            rim_rows(s2, cr2, g)
            insert(s2, cr2, g)

    for c in weights[6:]:
        c.wait()
    rims_in("two_2", (2,))
    def two(h0):
        acc[rows_of(h0), :] = dot(s2, t2, ((2, 1),), h0)
        pair[rows_of(h0), LATE] = dot(s2, t2, ((2, 3),), h0, lanes=LATE)
    blocks(two)
    rims_in("two_3", (3,))
    def three(h0):
        acc[rows_of(h0), :] += dot(s2, t2, ((3, 2),), h0)
    blocks(three)
    rims_in("two_01", (0, 1))

    def outer(h0):
        d = dot(s2, t2, ((0, 1), (1, 2)), h0)
        finish(d[:, EARLY], 0, h0)
        finish(d[:, LATE] + pair[rows_of(h0), LATE], 1, h0)
    blocks(outer)

    def one(h0):
        finish(acc[rows_of(h0), EARLY] + dot(s2, t2, ((1, 0),), h0, lanes=EARLY), 2, h0)
    blocks(one)

    wait_rims("two_cut")
    for i in range(3):
        face2_copy(i).wait_recv()
    def face_shift(k, _):
        a = s2[T, pl.ds(1 + R * k, R), :, MID].astype(F32)
        shifted(s2, T, 1 + R * k, R, a)
        return 0
    lax.fori_loop(0, H // R, face_shift, 0)
    rim_rows(s2, cr2, T)
    insert(s2, cr2, T)

    def last(h0):
        finish(acc[rows_of(h0), LATE] + dot(s2, t2, ((T, 3),), h0, lanes=LATE), 3, h0)
    blocks(last)

    for group in groups:
        wait_lines(send.at[names.index(group)], lines(group))
    for i in range(3):
        face_copy(i).wait_send()
        face2_copy(i).wait_send()


def place(x_ref, o_ref, sem):
    c = pltpu.make_async_copy(x_ref, o_ref, sem.at[0])
    c.start()
    c.wait()


def body(features, kernel_one, kernel_two):
    out = pl.pallas_call(
        kernel,
        out_shape=jax.ShapeDtypeStruct((T, H, W, C), BF16),
        in_specs=[pl.BlockSpec(memory_space=pltpu.HBM)] * 3,
        out_specs=pl.BlockSpec(memory_space=pltpu.VMEM),
        scratch_shapes=[
            pltpu.VMEM((T, H, W, C), BF16),
            pltpu.VMEM((H, W, C), BF16),
            pltpu.VMEM((2, T + 1, W, C), BF16),
            pltpu.VMEM((T + 1, H + 2, W, 3 * C), BF16),
            pltpu.VMEM((T + 1, H + 2, W, 3 * C), BF16),
            pltpu.VMEM((4, 9, C, 2 * C), BF16),
            pltpu.VMEM((4, 9, C, 2 * C), BF16),
            pltpu.VMEM((H * W, 2 * C), F32),
            pltpu.VMEM((H * W, 2 * C), F32),
            pltpu.VMEM((2, T, H, 1, C), F32),
            pltpu.VMEM((2, T + 1, H + 2, 1, C), F32),
            pltpu.VMEM((2, T, H, 1, C), F32),
            pltpu.VMEM((2, T + 1, H + 2, 1, C), F32),
            pltpu.VMEM((R, W + 16, C), F32),
            pltpu.VMEM((288, 1, C), F32),
            pltpu.SemaphoreType.DMA((14,)),
            pltpu.SemaphoreType.DMA((14,)),
            pltpu.SemaphoreType.DMA((T + 12,)),
        ],
        compiler_params=pltpu.CompilerParams(
            collective_id=0, has_side_effects=True, vmem_limit_bytes=26 << 20),
        name="resblock",
    )(*(pltpu.with_memory_space_constraint(a, pltpu.HBM) for a in (
        features, kernel_one.reshape(3, 9, C, C), kernel_two.reshape(3, 9, C, C))))
    return pl.pallas_call(
        place, out_shape=jax.ShapeDtypeStruct((T, H, W, C), BF16),
        in_specs=[pl.BlockSpec(memory_space=pl.ANY)], out_specs=pl.BlockSpec(memory_space=pl.ANY),
        scratch_shapes=[pltpu.SemaphoreType.DMA((1,))],
        compiler_params=pltpu.CompilerParams(vmem_limit_bytes=1 << 20), name="place")(out)


def solution(mesh):
    return jax.shard_map(
        body,
        mesh=mesh,
        in_specs=(P("ta", "ha", "wa", None), P(), P()),
        out_specs=P("ta", "ha", "wa", None),
        check_vma=False,
    )
```

```python
import jax
import jax.numpy as jnp
from jax import lax
from jax.experimental import pallas as pl
from jax.experimental.pallas import tpu as pltpu
from jax.sharding import PartitionSpec as P

MESH = pl.DeviceIdType.MESH
F32, BF16 = jnp.float32, jnp.bfloat16
T, H, W, C = 4, 32, 32, 128
R = 16
DIRS = [(dh, dw) for dh in (-1, 0, 1) for dw in (-1, 0, 1) if (dh, dw) != (0, 0)]
ROWS = [d for d in DIRS if d[1] == 0]
COLUMNS = [d for d in DIRS if d[1] != 0]
LEFT, MID, RIGHT = slice(0, C), slice(C, 2 * C), slice(2 * C, 3 * C)
EARLY, LATE, BOTH = slice(0, C), slice(C, 2 * C), slice(0, 2 * C)


def normed_silu(v):
    half = v * lax.rsqrt(jnp.sum(v * v, axis=-1, keepdims=True) * (4.0 / C) + 4e-06)
    return half + half * jnp.tanh(half)


def kernel(x_hbm, k1_hbm, k2_hbm, o_ref, xv, face, halo, s1, s2, t1, t2, acc, pair,
           cs1, cr1, cs2, cr2, shift, bytes_of, send, recv, local):
    ta, ha, wa = (lax.axis_index(a) for a in ("ta", "ha", "wa"))
    nh, nw = lax.axis_size("ha"), lax.axis_size("wa")

    def frame(g):
        return g + ta * (3 - 2 * g)

    def device(d, flip):
        return {"ta": 1 - ta if flip else ta, "ha": lax.rem(ha + d[0] + nh, nh),
                "wa": lax.rem(wa + d[1] + nw, nw)}

    def remote(src, dst, r, dev):
        return pltpu.make_async_remote_copy(
            src_ref=src, dst_ref=dst, send_sem=send.at[r], recv_sem=recv.at[r],
            device_id=dev, device_id_type=MESH)

    side = {-1: 0, 1: 1}

    groups = {
        "raw": (x_hbm, None, pl.ds(0, T), T, False),
        "raw_cut": (x_hbm, None, T, 1, True),
        "one": (s1, pl.ds(0, T), pl.ds(0, T), T, False),
        "one_cut": (s1, 3, T, 1, True),
        "two_2": (s2, 2, 2, 1, False),
        "two_3": (s2, 3, 3, 1, False),
        "two_cut": (s2, 3, T, 1, True),
        "two_01": (s2, pl.ds(0, 2), pl.ds(0, 2), 2, False),
    }
    names = list(groups)

    def dirs_of(group):
        return ROWS if "raw" in group else COLUMNS if "one" in group else DIRS

    def start_rims(group):
        source, mine, theirs, _, flip = groups[group]
        cs, cr = (cs2, cr2) if source is s2 else (cs1, cr1)
        for dh, dw in dirs_of(group):
            row = 0 if dh < 0 else H - 1
            slot = H + 1 if dh < 0 else 0
            if dw == 0 and source is x_hbm:
                src = x_hbm.at[frame(3), row] if flip else x_hbm.at[:, row]
                dst = halo.at[side[-dh], theirs]
            elif dw == 0:
                src = s2.at[mine, row + 1, :, pl.ds(C, C)]
                dst = s2.at[theirs, slot, :, pl.ds(C, C)]
            elif dh == 0:
                src = cs.at[side[dw], mine]
                dst = cr.at[side[-dw], theirs, pl.ds(1, H)]
            else:
                src = cs.at[side[dw], mine, row]
                dst = cr.at[side[-dw], theirs, slot]
            remote(src, dst, names.index(group), device((dh, dw), flip)).start()

    def lines(group):
        n = groups[group][3]
        rows, columns = 2 * n * W // 2, 2 * n * (H + 2)
        return rows if "raw" in group else columns if "one" in group else rows + columns

    def wait_lines(sem, n):
        pltpu.make_async_copy(bytes_of.at[pl.ds(0, n)], bytes_of.at[pl.ds(0, n)], sem).wait()

    def wait_rims(group):
        wait_lines(recv.at[names.index(group)], lines(group))

    partner = {"ta": 1 - ta, "ha": ha, "wa": wa}
    cuts = [(0, 8), (8, R - 7), (R + 1, H - R - 1)]
    cuts2 = [(0, R), (R, 8), (R + 8, 8)]

    def face_copy(i):
        a, n = cuts[i]
        return remote(x_hbm.at[frame(3), pl.ds(a, n)], face.at[pl.ds(a, n)], 8 + i, partner)

    def face2_copy(i):
        rows = pl.ds(1 + cuts2[i][0], cuts2[i][1])
        return remote(s2.at[3, rows, :, pl.ds(C, C)], s2.at[T, rows, :, pl.ds(C, C)], 11 + i, partner)

    loads = [pltpu.make_async_copy(x_hbm.at[frame(g)], xv.at[frame(g)], local.at[g])
             for g in range(T)]
    for c in loads[::-1]:
        c.start()
    weights = []
    for n, (k, t) in enumerate(((k1_hbm, t1), (k2_hbm, t2))):
        for i in range(3):
            tap = 1 + (i - 1) * (1 - 2 * ta)
            for part in range(2):
                weights.append(pltpu.make_async_copy(
                    k.at[tap], t.at[i + part, :, :, pl.ds(C * part, C)],
                    local.at[T + 6 * n + 2 * i + part]))
    for c in weights[:6]:
        c.start()

    barrier = pltpu.get_barrier_semaphore()
    for d in DIRS:
        for flip in (False, True):
            pl.semaphore_signal(barrier, inc=1, device_id=device(d, flip), device_id_type=MESH)
    pl.semaphore_signal(barrier, inc=1, device_id=partner, device_id_type=MESH)
    for t in (t1, t2):
        t[0, :, :, LATE] = jnp.zeros((9, C, C), BF16)
        t[3, :, :, EARLY] = jnp.zeros((9, C, C), BF16)
    shift[:, 0:8] = jnp.zeros((R, 8, C), F32)
    shift[:, 8 + W:] = jnp.zeros((R, 8, C), F32)
    inside = ((0, ha > 0), (H + 1, ha < nh - 1))
    first_column = jnp.where(wa > 0, 0, -1)
    last_column = jnp.where(wa < nw - 1, 15, -1)

    before = 7 + lax.div(ta, 2)
    after = before + 2

    def shifted(s, g, r0, n, a):
        rows = pl.ds(r0, n)
        shift[0:n, 8:8 + W] = a
        s[g, rows, :, LEFT] = shift[0:n, pl.ds(before, W)].astype(BF16)
        s[g, rows, :, RIGHT] = shift[0:n, pl.ds(after, W)].astype(BF16)

    def spread(s, g, r0, n, a):
        s[g, pl.ds(r0, n), :, MID] = a.astype(BF16)
        shifted(s, g, r0, n, a)

    def edges(cs, g, r0, n, a):
        cs[0, g, pl.ds(r0, n)] = a[:, 0:1, :]
        cs[1, g, pl.ds(r0, n)] = a[:, W - 1:W, :]

    def rim_rows(s, cr, g):
        for r, there in inside:
            rows = pl.ds(r, 1)
            a = s[g, rows, :, MID].astype(F32)
            column = lax.broadcasted_iota(jnp.int32, a.shape, 1)
            left = jnp.where(column == 0, jnp.where(wa > 0, cr[0, g, rows], 0.0), pltpu.roll(a, 1, 1))
            right = jnp.where(column == W - 1, jnp.where(wa < nw - 1, cr[1, g, rows], 0.0),
                              pltpu.roll(a, W - 1, 1))
            for lanes, v in ((LEFT, left), (MID, a), (RIGHT, right)):
                s[g, rows, :, lanes] = jnp.where(there, v, 0.0).astype(BF16)

    def insert(s, cr, g):
        def step(i, _):
            rows = pl.ds(1 + 16 * i, 16)
            line = lax.broadcasted_iota(jnp.int32, (16, 16, C), 1)
            left = s[g, rows, 0:16, LEFT].astype(F32)
            s[g, rows, 0:16, LEFT] = jnp.where(line == first_column, cr[0, g, rows], left).astype(BF16)
            right = s[g, rows, 16:32, RIGHT].astype(F32)
            s[g, rows, 16:32, RIGHT] = jnp.where(line == last_column, cr[1, g, rows], right).astype(BF16)
            return 0
        lax.fori_loop(0, 2, step, 0)

    def dot(s, t, pairs, h0, columns=(0, 1, 2), lanes=BOTH):
        parts, taps = [], []
        for f, j in pairs:
            for kh in range(3):
                rows = pl.ds(h0 + kh, R)
                for kw in columns:
                    parts.append(s[f, rows, :, kw * C:(kw + 1) * C].reshape(R * W, C))
                    taps.append(t[j, 3 * kh + kw, :, lanes])
        return jnp.dot(jnp.concatenate(parts, axis=1), jnp.concatenate(taps, axis=0),
                       preferred_element_type=F32)

    def rows_of(h0, n=R):
        return pl.ds(h0 * W if isinstance(h0, int) else pl.multiple_of(h0 * W, n * W), n * W)

    def activate(sums, lanes, g, h0):
        def step(i, _):
            r = h0 + R * i
            hid = sums[rows_of(r, R), lanes]
            a = normed_silu(hid.astype(BF16).astype(F32)).reshape(R, W, C)
            spread(s2, g, 1 + r, R, a)
            edges(cs2, g, r, R, a)
            return 0
        lax.fori_loop(0, 1, step, 0)

    def finish(out, g, h0):
        rows = pl.ds(h0, R)
        o_ref[frame(g), rows] = (xv[frame(g), rows].astype(F32) + out.reshape(R, W, C)).astype(BF16)

    def blocks(step):
        lax.fori_loop(0, H // R, lambda i, _: step(i * R) or 0, 0)

    def outer_columns(g):
        loads[g].wait()
        for k in range(2):
            a = normed_silu(xv[frame(g), :, 24 * k:24 * k + 8].astype(F32))
            cs1[k, g] = a[:, 7 * k:7 * k + 1, :]

    for g in (3, 2, 1, 0):
        outer_columns(g)
    pl.semaphore_wait(barrier, 2 * len(DIRS) + 1)

    start_rims("raw")
    start_rims("raw_cut")
    start_rims("one")
    start_rims("one_cut")
    face_copy(0).start()
    for i in (1, 2):
        face_copy(i).start()
    for c in weights[6:]:
        c.start()

    def first_act(i, _):
        g, r = i // 2, R * (i % 2)
        spread(s1, g, 1 + r, R, normed_silu(xv[frame(g), pl.ds(r, R)].astype(F32)))
        return 0
    lax.fori_loop(0, 2 * T, first_act, 0)

    def halo_rows(g, at):
        for k in range(2):
            a = jnp.where(inside[k][1], normed_silu(halo[k, at].astype(F32)), 0.0)
            s1[g, inside[k][0], :, MID] = a.astype(BF16)

    wait_rims("raw")
    for g in range(T):
        halo_rows(g, frame(g))
    for c in weights[:6]:
        c.wait()

    def middle(h0):
        acc[rows_of(h0), :] = dot(s1, t1, ((1, 0), (2, 1), (3, 2)), h0, (1,))
        pair[rows_of(h0), :] = dot(s1, t1, ((0, 1), (1, 2), (2, 3)), h0, (1,))
    blocks(middle)
    wait_rims("one")
    for g in range(T):
        rim_rows(s1, cr1, g)
        insert(s1, cr1, g)

    def inner(h0):
        acc[rows_of(h0), :] += dot(s1, t1, ((1, 0), (2, 1), (3, 2)), h0, (0, 2))
        activate(acc, EARLY, 2, h0)
    blocks(inner)
    start_rims("two_2")
    wait_rims("raw_cut")
    halo_rows(T, T)
    wait_rims("one_cut")
    rim_rows(s1, cr1, T)

    def cut_block(i):
        h0 = i * R
        for piece in ((0, 1), (2,))[i]:
            face_copy(piece).wait_recv()
        r0 = (0, R + 1)[i]
        for r, n in ((r0, 8), (r0 + 8, 9 if i == 0 else 7)):
            spread(s1, T, 1 + r, n, normed_silu(face[pl.ds(r, n)].astype(F32)))
        insert(s1, cr1, T)
        acc[rows_of(h0), LATE] += dot(s1, t1, ((T, 3),), h0, lanes=LATE)
        activate(acc, LATE, 3, h0)

    def outer_block(h0):
        pair[rows_of(h0), :] += dot(s1, t1, ((0, 1), (1, 2), (2, 3)), h0, (0, 2))
        activate(pair, EARLY, 0, h0)
        activate(pair, LATE, 1, h0)

    cut_block(0)
    face2_copy(0).start()
    cut_block(1)
    start_rims("two_3")
    start_rims("two_cut")
    blocks(outer_block)
    start_rims("two_01")
    face2_copy(1).start()
    face2_copy(2).start()

    def rims_in(group, frames):
        wait_rims(group)
        for g in frames:
            rim_rows(s2, cr2, g)
            insert(s2, cr2, g)

    for c in weights[6:]:
        c.wait()
    rims_in("two_2", (2,))
    def two(h0):
        acc[rows_of(h0), :] = dot(s2, t2, ((2, 1),), h0)
        pair[rows_of(h0), LATE] = dot(s2, t2, ((2, 3),), h0, lanes=LATE)
    blocks(two)
    rims_in("two_3", (3,))
    def three(h0):
        acc[rows_of(h0), :] += dot(s2, t2, ((3, 2),), h0)
    blocks(three)
    rims_in("two_01", (0, 1))

    def outer(h0):
        d = dot(s2, t2, ((0, 1), (1, 2)), h0)
        finish(d[:, EARLY], 0, h0)
        finish(d[:, LATE] + pair[rows_of(h0), LATE], 1, h0)
    blocks(outer)

    def one(h0):
        finish(acc[rows_of(h0), EARLY] + dot(s2, t2, ((1, 0),), h0, lanes=EARLY), 2, h0)
    blocks(one)

    wait_rims("two_cut")
    for i in range(3):
        face2_copy(i).wait_recv()
    def face_shift(k, _):
        a = s2[T, pl.ds(1 + R * k, R), :, MID].astype(F32)
        shifted(s2, T, 1 + R * k, R, a)
        return 0
    lax.fori_loop(0, H // R, face_shift, 0)
    rim_rows(s2, cr2, T)
    insert(s2, cr2, T)

    def last(h0):
        finish(acc[rows_of(h0), LATE] + dot(s2, t2, ((T, 3),), h0, lanes=LATE), 3, h0)
    blocks(last)

    for group in groups:
        wait_lines(send.at[names.index(group)], lines(group))
    for i in range(3):
        face_copy(i).wait_send()
        face2_copy(i).wait_send()


def place(x_ref, o_ref, sem):
    c = pltpu.make_async_copy(x_ref, o_ref, sem.at[0])
    c.start()
    c.wait()


def body(features, kernel_one, kernel_two):
    out = pl.pallas_call(
        kernel,
        out_shape=jax.ShapeDtypeStruct((T, H, W, C), BF16),
        in_specs=[pl.BlockSpec(memory_space=pltpu.HBM)] * 3,
        out_specs=pl.BlockSpec(memory_space=pltpu.VMEM),
        scratch_shapes=[
            pltpu.VMEM((T, H, W, C), BF16),
            pltpu.VMEM((H, W, C), BF16),
            pltpu.VMEM((2, T + 1, W, C), BF16),
            pltpu.VMEM((T + 1, H + 2, W, 3 * C), BF16),
            pltpu.VMEM((T + 1, H + 2, W, 3 * C), BF16),
            pltpu.VMEM((4, 9, C, 2 * C), BF16),
            pltpu.VMEM((4, 9, C, 2 * C), BF16),
            pltpu.VMEM((H * W, 2 * C), F32),
            pltpu.VMEM((H * W, 2 * C), F32),
            pltpu.VMEM((2, T, H, 1, C), F32),
            pltpu.VMEM((2, T + 1, H + 2, 1, C), F32),
            pltpu.VMEM((2, T, H, 1, C), F32),
            pltpu.VMEM((2, T + 1, H + 2, 1, C), F32),
            pltpu.VMEM((R, W + 16, C), F32),
            pltpu.VMEM((288, 1, C), F32),
            pltpu.SemaphoreType.DMA((14,)),
            pltpu.SemaphoreType.DMA((14,)),
            pltpu.SemaphoreType.DMA((T + 12,)),
        ],
        compiler_params=pltpu.CompilerParams(
            collective_id=0, has_side_effects=True, vmem_limit_bytes=26 << 20),
        name="resblock",
    )(*(pltpu.with_memory_space_constraint(a, pltpu.HBM) for a in (
        features, kernel_one.reshape(3, 9, C, C), kernel_two.reshape(3, 9, C, C))))
    return pl.pallas_call(
        place, out_shape=jax.ShapeDtypeStruct((T, H, W, C), BF16),
        in_specs=[pl.BlockSpec(memory_space=pl.ANY)], out_specs=pl.BlockSpec(memory_space=pl.ANY),
        scratch_shapes=[pltpu.SemaphoreType.DMA((1,))],
        compiler_params=pltpu.CompilerParams(vmem_limit_bytes=1 << 20), name="place")(out)


def solution(mesh):
    return jax.shard_map(
        body,
        mesh=mesh,
        in_specs=(P("ta", "ha", "wa", None), P(), P()),
        out_specs=P("ta", "ha", "wa", None),
        check_vma=False,
    )
```

```python
import jax
import jax.numpy as jnp
from jax import lax
from jax.experimental import pallas as pl
from jax.experimental.pallas import tpu as pltpu
from jax.sharding import PartitionSpec as P

MESH = pl.DeviceIdType.MESH
F32, BF16 = jnp.float32, jnp.bfloat16
T, H, W, C = 4, 32, 32, 128
R = 16
DIRS = [(dh, dw) for dh in (-1, 0, 1) for dw in (-1, 0, 1) if (dh, dw) != (0, 0)]
ROWS = [d for d in DIRS if d[1] == 0]
COLUMNS = [d for d in DIRS if d[1] != 0]
LEFT, MID, RIGHT = slice(0, C), slice(C, 2 * C), slice(2 * C, 3 * C)
EARLY, LATE, BOTH = slice(0, C), slice(C, 2 * C), slice(0, 2 * C)


def normed_silu(v):
    half = v * lax.rsqrt(jnp.sum(v * v, axis=-1, keepdims=True) * (4.0 / C) + 4e-06)
    return half + half * jnp.tanh(half)


def kernel(x_hbm, k1_hbm, k2_hbm, o_ref, xv, face, halo, s1, s2, t1, t2, acc, pair,
           cs1, cr1, cs2, cr2, shift, bytes_of, send, recv, local):
    ta, ha, wa = (lax.axis_index(a) for a in ("ta", "ha", "wa"))
    nh, nw = lax.axis_size("ha"), lax.axis_size("wa")

    def frame(g):
        return g + ta * (3 - 2 * g)

    def device(d, flip):
        return {"ta": 1 - ta if flip else ta, "ha": lax.rem(ha + d[0] + nh, nh),
                "wa": lax.rem(wa + d[1] + nw, nw)}

    def remote(src, dst, r, dev):
        return pltpu.make_async_remote_copy(
            src_ref=src, dst_ref=dst, send_sem=send.at[r], recv_sem=recv.at[r],
            device_id=dev, device_id_type=MESH)

    side = {-1: 0, 1: 1}

    groups = {
        "raw": (x_hbm, None, pl.ds(0, T), T, False),
        "raw_cut": (x_hbm, None, T, 1, True),
        "one": (s1, pl.ds(0, T), pl.ds(0, T), T, False),
        "one_cut": (s1, 3, T, 1, True),
        "two_2": (s2, 2, 2, 1, False),
        "two_3": (s2, 3, 3, 1, False),
        "two_cut": (s2, 3, T, 1, True),
        "two_01": (s2, pl.ds(0, 2), pl.ds(0, 2), 2, False),
    }
    names = list(groups)

    def dirs_of(group):
        return ROWS if "raw" in group else COLUMNS if "one" in group else DIRS

    def start_rims(group):
        source, mine, theirs, _, flip = groups[group]
        cs, cr = (cs2, cr2) if source is s2 else (cs1, cr1)
        for dh, dw in dirs_of(group):
            row = 0 if dh < 0 else H - 1
            slot = H + 1 if dh < 0 else 0
            if dw == 0 and source is x_hbm:
                src = x_hbm.at[frame(3), row] if flip else x_hbm.at[:, row]
                dst = halo.at[side[-dh], theirs]
            elif dw == 0:
                src = s2.at[mine, row + 1, :, pl.ds(C, C)]
                dst = s2.at[theirs, slot, :, pl.ds(C, C)]
            elif dh == 0:
                src = cs.at[side[dw], mine]
                dst = cr.at[side[-dw], theirs, pl.ds(1, H)]
            else:
                src = cs.at[side[dw], mine, row]
                dst = cr.at[side[-dw], theirs, slot]
            remote(src, dst, names.index(group), device((dh, dw), flip)).start()

    def lines(group):
        n = groups[group][3]
        rows, columns = 2 * n * W // 2, 2 * n * (H + 2)
        return rows if "raw" in group else columns if "one" in group else rows + columns

    def wait_lines(sem, n):
        pltpu.make_async_copy(bytes_of.at[pl.ds(0, n)], bytes_of.at[pl.ds(0, n)], sem).wait()

    def wait_rims(group):
        wait_lines(recv.at[names.index(group)], lines(group))

    partner = {"ta": 1 - ta, "ha": ha, "wa": wa}
    cuts = [(0, 8), (8, R - 7), (R + 1, H - R - 1)]
    cuts2 = [(0, 8), (8, 12), (20, 12)]

    def face_copy(i):
        a, n = cuts[i]
        return remote(x_hbm.at[frame(3), pl.ds(a, n)], face.at[pl.ds(a, n)], 8 + i, partner)

    def face2_copy(i):
        rows = pl.ds(1 + cuts2[i][0], cuts2[i][1])
        return remote(s2.at[3, rows, :, pl.ds(C, C)], s2.at[T, rows, :, pl.ds(C, C)], 11 + i, partner)

    loads = [pltpu.make_async_copy(x_hbm.at[frame(g)], xv.at[frame(g)], local.at[g])
             for g in range(T)]
    for c in loads[::-1]:
        c.start()
    weights = []
    for n, (k, t) in enumerate(((k1_hbm, t1), (k2_hbm, t2))):
        for i in range(3):
            tap = 1 + (i - 1) * (1 - 2 * ta)
            for part in range(2):
                weights.append(pltpu.make_async_copy(
                    k.at[tap], t.at[i + part, :, :, pl.ds(C * part, C)],
                    local.at[T + 6 * n + 2 * i + part]))
    for c in weights[:6]:
        c.start()

    barrier = pltpu.get_barrier_semaphore()
    for d in DIRS:
        for flip in (False, True):
            pl.semaphore_signal(barrier, inc=1, device_id=device(d, flip), device_id_type=MESH)
    pl.semaphore_signal(barrier, inc=1, device_id=partner, device_id_type=MESH)
    for t in (t1, t2):
        t[0, :, :, LATE] = jnp.zeros((9, C, C), BF16)
        t[3, :, :, EARLY] = jnp.zeros((9, C, C), BF16)
    shift[:, 0:8] = jnp.zeros((R, 8, C), F32)
    shift[:, 8 + W:] = jnp.zeros((R, 8, C), F32)
    inside = ((0, ha > 0), (H + 1, ha < nh - 1))
    first_column = jnp.where(wa > 0, 0, -1)
    last_column = jnp.where(wa < nw - 1, 15, -1)

    before = 7 + lax.div(ta, 2)
    after = before + 2

    def shifted(s, g, r0, n, a):
        rows = pl.ds(r0, n)
        shift[0:n, 8:8 + W] = a
        s[g, rows, :, LEFT] = shift[0:n, pl.ds(before, W)].astype(BF16)
        s[g, rows, :, RIGHT] = shift[0:n, pl.ds(after, W)].astype(BF16)

    def spread(s, g, r0, n, a):
        s[g, pl.ds(r0, n), :, MID] = a.astype(BF16)
        shifted(s, g, r0, n, a)

    def edges(cs, g, r0, n, a):
        cs[0, g, pl.ds(r0, n)] = a[:, 0:1, :]
        cs[1, g, pl.ds(r0, n)] = a[:, W - 1:W, :]

    def rim_rows(s, cr, g):
        for r, there in inside:
            rows = pl.ds(r, 1)
            a = s[g, rows, :, MID].astype(F32)
            column = lax.broadcasted_iota(jnp.int32, a.shape, 1)
            left = jnp.where(column == 0, jnp.where(wa > 0, cr[0, g, rows], 0.0), pltpu.roll(a, 1, 1))
            right = jnp.where(column == W - 1, jnp.where(wa < nw - 1, cr[1, g, rows], 0.0),
                              pltpu.roll(a, W - 1, 1))
            for lanes, v in ((LEFT, left), (MID, a), (RIGHT, right)):
                s[g, rows, :, lanes] = jnp.where(there, v, 0.0).astype(BF16)

    def insert(s, cr, g):
        def step(i, _):
            rows = pl.ds(1 + 32 * i, 32)
            line = lax.broadcasted_iota(jnp.int32, (32, 16, C), 1)
            left = s[g, rows, 0:16, LEFT].astype(F32)
            s[g, rows, 0:16, LEFT] = jnp.where(line == first_column, cr[0, g, rows], left).astype(BF16)
            right = s[g, rows, 16:32, RIGHT].astype(F32)
            s[g, rows, 16:32, RIGHT] = jnp.where(line == last_column, cr[1, g, rows], right).astype(BF16)
            return 0
        step(0, 0)

    def dot(s, t, pairs, h0, columns=(0, 1, 2), lanes=BOTH):
        parts, taps = [], []
        for f, j in pairs:
            for kh in range(3):
                rows = pl.ds(h0 + kh, R)
                for kw in columns:
                    parts.append(s[f, rows, :, kw * C:(kw + 1) * C].reshape(R * W, C))
                    taps.append(t[j, 3 * kh + kw, :, lanes])
        return jnp.dot(jnp.concatenate(parts, axis=1), jnp.concatenate(taps, axis=0),
                       preferred_element_type=F32)

    def rows_of(h0, n=R):
        return pl.ds(h0 * W if isinstance(h0, int) else pl.multiple_of(h0 * W, n * W), n * W)

    def activate(sums, lanes, g, h0):
        def step(i, _):
            r = h0 + R * i
            hid = sums[rows_of(r, R), lanes]
            a = normed_silu(hid.astype(BF16).astype(F32)).reshape(R, W, C)
            spread(s2, g, 1 + r, R, a)
            edges(cs2, g, r, R, a)
            return 0
        lax.fori_loop(0, 1, step, 0)

    def finish(out, g, h0):
        rows = pl.ds(h0, R)
        o_ref[frame(g), rows] = (xv[frame(g), rows].astype(F32) + out.reshape(R, W, C)).astype(BF16)

    def blocks(step):
        lax.fori_loop(0, H // R, lambda i, _: step(i * R) or 0, 0)

    def outer_columns(g):
        loads[g].wait()
        for k in range(2):
            a = normed_silu(xv[frame(g), :, 24 * k:24 * k + 8].astype(F32))
            cs1[k, g] = a[:, 7 * k:7 * k + 1, :]

    for g in (3, 2, 1, 0):
        outer_columns(g)
    pl.semaphore_wait(barrier, 2 * len(DIRS) + 1)

    start_rims("raw")
    start_rims("raw_cut")
    start_rims("one")
    start_rims("one_cut")
    face_copy(0).start()
    for i in (1, 2):
        face_copy(i).start()
    for c in weights[6:]:
        c.start()

    def first_act(i, _):
        g, r = i // 2, R * (i % 2)
        spread(s1, g, 1 + r, R, normed_silu(xv[frame(g), pl.ds(r, R)].astype(F32)))
        return 0
    lax.fori_loop(0, 2 * T, first_act, 0)

    def halo_rows(g, at):
        for k in range(2):
            a = jnp.where(inside[k][1], normed_silu(halo[k, at].astype(F32)), 0.0)
            s1[g, inside[k][0], :, MID] = a.astype(BF16)

    wait_rims("raw")
    for g in range(T):
        halo_rows(g, frame(g))
    for c in weights[:6]:
        c.wait()

    def middle(h0):
        acc[rows_of(h0), :] = dot(s1, t1, ((1, 0), (2, 1), (3, 2)), h0, (1,))
        pair[rows_of(h0), :] = dot(s1, t1, ((0, 1), (1, 2), (2, 3)), h0, (1,))
    blocks(middle)
    wait_rims("one")
    for g in range(T):
        rim_rows(s1, cr1, g)
        insert(s1, cr1, g)

    def inner(h0):
        acc[rows_of(h0), :] += dot(s1, t1, ((1, 0), (2, 1), (3, 2)), h0, (0, 2))
        activate(acc, EARLY, 2, h0)
    blocks(inner)
    start_rims("two_2")
    wait_rims("raw_cut")
    halo_rows(T, T)
    wait_rims("one_cut")
    rim_rows(s1, cr1, T)

    def cut_block(i):
        h0 = i * R
        for piece in ((0, 1), (2,))[i]:
            face_copy(piece).wait_recv()
        r0 = (0, R + 1)[i]
        for r, n in ((r0, 8), (r0 + 8, 9 if i == 0 else 7)):
            spread(s1, T, 1 + r, n, normed_silu(face[pl.ds(r, n)].astype(F32)))
        insert(s1, cr1, T)
        acc[rows_of(h0), LATE] += dot(s1, t1, ((T, 3),), h0, lanes=LATE)
        activate(acc, LATE, 3, h0)

    def outer_block(h0):
        pair[rows_of(h0), :] += dot(s1, t1, ((0, 1), (1, 2), (2, 3)), h0, (0, 2))
        activate(pair, EARLY, 0, h0)
        activate(pair, LATE, 1, h0)

    cut_block(0)
    face2_copy(0).start()
    cut_block(1)
    start_rims("two_3")
    start_rims("two_cut")
    blocks(outer_block)
    start_rims("two_01")
    face2_copy(1).start()
    face2_copy(2).start()

    def rims_in(group, frames):
        wait_rims(group)
        for g in frames:
            rim_rows(s2, cr2, g)
            insert(s2, cr2, g)

    for c in weights[6:]:
        c.wait()
    rims_in("two_2", (2,))
    def two(h0):
        acc[rows_of(h0), :] = dot(s2, t2, ((2, 1),), h0)
        pair[rows_of(h0), LATE] = dot(s2, t2, ((2, 3),), h0, lanes=LATE)
    blocks(two)
    rims_in("two_3", (3,))
    def three(h0):
        acc[rows_of(h0), :] += dot(s2, t2, ((3, 2),), h0)
    blocks(three)
    rims_in("two_01", (0, 1))

    def outer(h0):
        d = dot(s2, t2, ((0, 1), (1, 2)), h0)
        finish(d[:, EARLY], 0, h0)
        finish(d[:, LATE] + pair[rows_of(h0), LATE], 1, h0)
    blocks(outer)

    def one(h0):
        finish(acc[rows_of(h0), EARLY] + dot(s2, t2, ((1, 0),), h0, lanes=EARLY), 2, h0)
    blocks(one)

    wait_rims("two_cut")
    for i in range(3):
        face2_copy(i).wait_recv()
    def face_shift(k, _):
        a = s2[T, pl.ds(1 + R * k, R), :, MID].astype(F32)
        shifted(s2, T, 1 + R * k, R, a)
        return 0
    lax.fori_loop(0, H // R, face_shift, 0)
    rim_rows(s2, cr2, T)
    insert(s2, cr2, T)

    def last(h0):
        finish(acc[rows_of(h0), LATE] + dot(s2, t2, ((T, 3),), h0, lanes=LATE), 3, h0)
    blocks(last)

    for group in groups:
        wait_lines(send.at[names.index(group)], lines(group))
    for i in range(3):
        face_copy(i).wait_send()
        face2_copy(i).wait_send()


def place(x_ref, o_ref, sem):
    copies = [pltpu.make_async_copy(x_ref.at[g], o_ref.at[g], sem.at[g]) for g in range(T)]
    for c in copies:
        c.start()
    for c in copies:
        c.wait()


def body(features, kernel_one, kernel_two):
    out = pl.pallas_call(
        kernel,
        out_shape=jax.ShapeDtypeStruct((T, H, W, C), BF16),
        in_specs=[pl.BlockSpec(memory_space=pltpu.HBM)] * 3,
        out_specs=pl.BlockSpec(memory_space=pltpu.VMEM),
        scratch_shapes=[
            pltpu.VMEM((T, H, W, C), BF16),
            pltpu.VMEM((H, W, C), BF16),
            pltpu.VMEM((2, T + 1, W, C), BF16),
            pltpu.VMEM((T + 1, H + 2, W, 3 * C), BF16),
            pltpu.VMEM((T + 1, H + 2, W, 3 * C), BF16),
            pltpu.VMEM((4, 9, C, 2 * C), BF16),
            pltpu.VMEM((4, 9, C, 2 * C), BF16),
            pltpu.VMEM((H * W, 2 * C), F32),
            pltpu.VMEM((H * W, 2 * C), F32),
            pltpu.VMEM((2, T, H, 1, C), F32),
            pltpu.VMEM((2, T + 1, H + 2, 1, C), F32),
            pltpu.VMEM((2, T, H, 1, C), F32),
            pltpu.VMEM((2, T + 1, H + 2, 1, C), F32),
            pltpu.VMEM((R, W + 16, C), F32),
            pltpu.VMEM((288, 1, C), F32),
            pltpu.SemaphoreType.DMA((14,)),
            pltpu.SemaphoreType.DMA((14,)),
            pltpu.SemaphoreType.DMA((T + 12,)),
        ],
        compiler_params=pltpu.CompilerParams(
            collective_id=0, has_side_effects=True, vmem_limit_bytes=26 << 20),
        name="resblock",
    )(*(pltpu.with_memory_space_constraint(a, pltpu.HBM) for a in (
        features, kernel_one.reshape(3, 9, C, C), kernel_two.reshape(3, 9, C, C))))
    return pl.pallas_call(
        place, out_shape=jax.ShapeDtypeStruct((T, H, W, C), BF16),
        in_specs=[pl.BlockSpec(memory_space=pl.ANY)], out_specs=pl.BlockSpec(memory_space=pl.ANY),
        scratch_shapes=[pltpu.SemaphoreType.DMA((T,))],
        compiler_params=pltpu.CompilerParams(vmem_limit_bytes=1 << 20), name="place")(out)


def solution(mesh):
    return jax.shard_map(
        body,
        mesh=mesh,
        in_specs=(P("ta", "ha", "wa", None), P(), P()),
        out_specs=P("ta", "ha", "wa", None),
        check_vma=False,
    )
```

```python
import jax
import jax.numpy as jnp
from jax import lax
from jax.experimental import pallas as pl
from jax.experimental.pallas import tpu as pltpu
from jax.sharding import PartitionSpec as P

MESH = pl.DeviceIdType.MESH
F32, BF16 = jnp.float32, jnp.bfloat16
T, H, W, C = 4, 32, 32, 128
R = 16
DIRS = [(dh, dw) for dh in (-1, 0, 1) for dw in (-1, 0, 1) if (dh, dw) != (0, 0)]
ROWS = [d for d in DIRS if d[1] == 0]
COLUMNS = [d for d in DIRS if d[1] != 0]
LEFT, MID, RIGHT = slice(0, C), slice(C, 2 * C), slice(2 * C, 3 * C)
EARLY, LATE, BOTH = slice(0, C), slice(C, 2 * C), slice(0, 2 * C)


def normed_silu(v):
    half = v * lax.rsqrt(jnp.sum(v * v, axis=-1, keepdims=True) * (4.0 / C) + 4e-06)
    return half + half * jnp.tanh(half)


def kernel(x_hbm, k1_hbm, k2_hbm, o_ref, xv, face, halo, s1, s2, t1, t2, acc, pair,
           cs1, cr1, cs2, cr2, shift, bytes_of, send, recv, local):
    ta, ha, wa = (lax.axis_index(a) for a in ("ta", "ha", "wa"))
    nh, nw = lax.axis_size("ha"), lax.axis_size("wa")

    def frame(g):
        return g + ta * (3 - 2 * g)

    def device(d, flip):
        return {"ta": 1 - ta if flip else ta, "ha": lax.rem(ha + d[0] + nh, nh),
                "wa": lax.rem(wa + d[1] + nw, nw)}

    def remote(src, dst, r, dev):
        return pltpu.make_async_remote_copy(
            src_ref=src, dst_ref=dst, send_sem=send.at[r], recv_sem=recv.at[r],
            device_id=dev, device_id_type=MESH)

    side = {-1: 0, 1: 1}

    groups = {
        "raw": (x_hbm, None, pl.ds(0, T), T, False),
        "raw_cut": (x_hbm, None, T, 1, True),
        "one": (s1, pl.ds(0, T), pl.ds(0, T), T, False),
        "one_cut": (s1, 3, T, 1, True),
        "two_2": (s2, 2, 2, 1, False),
        "two_3": (s2, 3, 3, 1, False),
        "two_cut": (s2, 3, T, 1, True),
        "two_01": (s2, pl.ds(0, 2), pl.ds(0, 2), 2, False),
    }
    names = list(groups)

    def dirs_of(group):
        return ROWS if "raw" in group else COLUMNS if "one" in group else DIRS

    def start_rims(group):
        source, mine, theirs, _, flip = groups[group]
        cs, cr = (cs2, cr2) if source is s2 else (cs1, cr1)
        for dh, dw in dirs_of(group):
            row = 0 if dh < 0 else H - 1
            slot = H + 1 if dh < 0 else 0
            if dw == 0 and source is x_hbm:
                src = x_hbm.at[frame(3), row] if flip else x_hbm.at[:, row]
                dst = halo.at[side[-dh], theirs]
            elif dw == 0:
                src = s2.at[mine, row + 1, :, pl.ds(C, C)]
                dst = s2.at[theirs, slot, :, pl.ds(C, C)]
            elif dh == 0:
                src = cs.at[side[dw], mine]
                dst = cr.at[side[-dw], theirs, pl.ds(1, H)]
            else:
                src = cs.at[side[dw], mine, row]
                dst = cr.at[side[-dw], theirs, slot]
            remote(src, dst, names.index(group), device((dh, dw), flip)).start()

    def lines(group):
        n = groups[group][3]
        rows, columns = 2 * n * W // 2, 2 * n * (H + 2)
        return rows if "raw" in group else columns if "one" in group else rows + columns

    def wait_lines(sem, n):
        pltpu.make_async_copy(bytes_of.at[pl.ds(0, n)], bytes_of.at[pl.ds(0, n)], sem).wait()

    def wait_rims(group):
        wait_lines(recv.at[names.index(group)], lines(group))

    partner = {"ta": 1 - ta, "ha": ha, "wa": wa}
    cuts = [(0, 8), (8, R - 7), (R + 1, H - R - 1)]
    cuts2 = [(0, 4), (4, 14), (18, 14)]

    def face_copy(i):
        a, n = cuts[i]
        return remote(x_hbm.at[frame(3), pl.ds(a, n)], face.at[pl.ds(a, n)], 8 + i, partner)

    def face2_copy(i):
        rows = pl.ds(1 + cuts2[i][0], cuts2[i][1])
        return remote(s2.at[3, rows, :, pl.ds(C, C)], s2.at[T, rows, :, pl.ds(C, C)], 11 + i, partner)

    loads = [pltpu.make_async_copy(x_hbm.at[frame(g)], xv.at[frame(g)], local.at[g])
             for g in range(T)]
    for c in loads[::-1]:
        c.start()
    weights = []
    for n, (k, t) in enumerate(((k1_hbm, t1), (k2_hbm, t2))):
        for i in range(3):
            tap = 1 + (i - 1) * (1 - 2 * ta)
            for part in range(2):
                weights.append(pltpu.make_async_copy(
                    k.at[tap], t.at[i + part, :, :, pl.ds(C * part, C)],
                    local.at[T + 6 * n + 2 * i + part]))
    for c in weights[:6]:
        c.start()

    barrier = pltpu.get_barrier_semaphore()
    for d in DIRS:
        for flip in (False, True):
            pl.semaphore_signal(barrier, inc=1, device_id=device(d, flip), device_id_type=MESH)
    pl.semaphore_signal(barrier, inc=1, device_id=partner, device_id_type=MESH)
    for t in (t1, t2):
        t[0, :, :, LATE] = jnp.zeros((9, C, C), BF16)
        t[3, :, :, EARLY] = jnp.zeros((9, C, C), BF16)
    shift[:, 0:8] = jnp.zeros((R, 8, C), F32)
    shift[:, 8 + W:] = jnp.zeros((R, 8, C), F32)
    inside = ((0, ha > 0), (H + 1, ha < nh - 1))
    first_column = jnp.where(wa > 0, 0, -1)
    last_column = jnp.where(wa < nw - 1, 15, -1)

    before = 7 + lax.div(ta, 2)
    after = before + 2

    def shifted(s, g, r0, n, a):
        rows = pl.ds(r0, n)
        shift[0:n, 8:8 + W] = a
        s[g, rows, :, LEFT] = shift[0:n, pl.ds(before, W)].astype(BF16)
        s[g, rows, :, RIGHT] = shift[0:n, pl.ds(after, W)].astype(BF16)

    def spread(s, g, r0, n, a):
        s[g, pl.ds(r0, n), :, MID] = a.astype(BF16)
        shifted(s, g, r0, n, a)

    def edges(cs, g, r0, n, a):
        cs[0, g, pl.ds(r0, n)] = a[:, 0:1, :]
        cs[1, g, pl.ds(r0, n)] = a[:, W - 1:W, :]

    def rim_rows(s, cr, g):
        for r, there in inside:
            rows = pl.ds(r, 1)
            a = s[g, rows, :, MID].astype(F32)
            column = lax.broadcasted_iota(jnp.int32, a.shape, 1)
            left = jnp.where(column == 0, jnp.where(wa > 0, cr[0, g, rows], 0.0), pltpu.roll(a, 1, 1))
            right = jnp.where(column == W - 1, jnp.where(wa < nw - 1, cr[1, g, rows], 0.0),
                              pltpu.roll(a, W - 1, 1))
            for lanes, v in ((LEFT, left), (MID, a), (RIGHT, right)):
                s[g, rows, :, lanes] = jnp.where(there, v, 0.0).astype(BF16)

    def insert(s, cr, g):
        def step(i, _):
            rows = pl.ds(1 + 32 * i, 32)
            line = lax.broadcasted_iota(jnp.int32, (32, 16, C), 1)
            left = s[g, rows, 0:16, LEFT].astype(F32)
            s[g, rows, 0:16, LEFT] = jnp.where(line == first_column, cr[0, g, rows], left).astype(BF16)
            right = s[g, rows, 16:32, RIGHT].astype(F32)
            s[g, rows, 16:32, RIGHT] = jnp.where(line == last_column, cr[1, g, rows], right).astype(BF16)
            return 0
        step(0, 0)

    def dot(s, t, pairs, h0, columns=(0, 1, 2), lanes=BOTH):
        parts, taps = [], []
        for f, j in pairs:
            for kh in range(3):
                rows = pl.ds(h0 + kh, R)
                for kw in columns:
                    parts.append(s[f, rows, :, kw * C:(kw + 1) * C].reshape(R * W, C))
                    taps.append(t[j, 3 * kh + kw, :, lanes])
        return jnp.dot(jnp.concatenate(parts, axis=1), jnp.concatenate(taps, axis=0),
                       preferred_element_type=F32)

    def rows_of(h0, n=R):
        return pl.ds(h0 * W if isinstance(h0, int) else pl.multiple_of(h0 * W, n * W), n * W)

    def activate(sums, lanes, g, h0):
        def step(i, _):
            r = h0 + R * i
            hid = sums[rows_of(r, R), lanes]
            a = normed_silu(hid.astype(BF16).astype(F32)).reshape(R, W, C)
            spread(s2, g, 1 + r, R, a)
            edges(cs2, g, r, R, a)
            return 0
        lax.fori_loop(0, 1, step, 0)

    def finish(out, g, h0):
        rows = pl.ds(h0, R)
        o_ref[frame(g), rows] = (xv[frame(g), rows].astype(F32) + out.reshape(R, W, C)).astype(BF16)

    def blocks(step):
        lax.fori_loop(0, H // R, lambda i, _: step(i * R) or 0, 0)

    def outer_columns(g):
        loads[g].wait()
        for k in range(2):
            a = normed_silu(xv[frame(g), :, 24 * k:24 * k + 8].astype(F32))
            cs1[k, g] = a[:, 7 * k:7 * k + 1, :]

    for g in (3, 2, 1, 0):
        outer_columns(g)
    pl.semaphore_wait(barrier, 2 * len(DIRS) + 1)

    start_rims("raw")
    start_rims("raw_cut")
    start_rims("one")
    start_rims("one_cut")
    face_copy(0).start()
    for i in (1, 2):
        face_copy(i).start()
    for c in weights[6:]:
        c.start()

    def first_act(i, _):
        g, r = i // 2, R * (i % 2)
        spread(s1, g, 1 + r, R, normed_silu(xv[frame(g), pl.ds(r, R)].astype(F32)))
        return 0
    lax.fori_loop(0, 2 * T, first_act, 0)

    def halo_rows(g, at):
        for k in range(2):
            a = jnp.where(inside[k][1], normed_silu(halo[k, at].astype(F32)), 0.0)
            s1[g, inside[k][0], :, MID] = a.astype(BF16)

    wait_rims("raw")
    for g in range(T):
        halo_rows(g, frame(g))
    for c in weights[:6]:
        c.wait()

    def middle(h0):
        acc[rows_of(h0), :] = dot(s1, t1, ((1, 0), (2, 1), (3, 2)), h0, (1,))
        pair[rows_of(h0), :] = dot(s1, t1, ((0, 1), (1, 2), (2, 3)), h0, (1,))
    blocks(middle)
    wait_rims("one")
    for g in range(T):
        rim_rows(s1, cr1, g)
        insert(s1, cr1, g)

    def inner(h0):
        acc[rows_of(h0), :] += dot(s1, t1, ((1, 0), (2, 1), (3, 2)), h0, (0, 2))
        activate(acc, EARLY, 2, h0)
    blocks(inner)
    start_rims("two_2")
    wait_rims("raw_cut")
    halo_rows(T, T)
    wait_rims("one_cut")
    rim_rows(s1, cr1, T)

    def cut_block(i):
        h0 = i * R
        for piece in ((0, 1), (2,))[i]:
            face_copy(piece).wait_recv()
        r0 = (0, R + 1)[i]
        for r, n in ((r0, 8), (r0 + 8, 9 if i == 0 else 7)):
            spread(s1, T, 1 + r, n, normed_silu(face[pl.ds(r, n)].astype(F32)))
        insert(s1, cr1, T)
        acc[rows_of(h0), LATE] += dot(s1, t1, ((T, 3),), h0, lanes=LATE)
        activate(acc, LATE, 3, h0)

    def outer_block(h0):
        pair[rows_of(h0), :] += dot(s1, t1, ((0, 1), (1, 2), (2, 3)), h0, (0, 2))
        activate(pair, EARLY, 0, h0)
        activate(pair, LATE, 1, h0)

    cut_block(0)
    face2_copy(0).start()
    cut_block(1)
    start_rims("two_3")
    start_rims("two_cut")
    blocks(outer_block)
    start_rims("two_01")
    face2_copy(1).start()
    face2_copy(2).start()

    def rims_in(group, frames):
        wait_rims(group)
        for g in frames:
            rim_rows(s2, cr2, g)
            insert(s2, cr2, g)

    for c in weights[6:]:
        c.wait()
    rims_in("two_2", (2,))
    def two(h0):
        acc[rows_of(h0), :] = dot(s2, t2, ((2, 1),), h0)
        pair[rows_of(h0), LATE] = dot(s2, t2, ((2, 3),), h0, lanes=LATE)
    blocks(two)
    rims_in("two_3", (3,))
    def three(h0):
        acc[rows_of(h0), :] += dot(s2, t2, ((3, 2),), h0)
    blocks(three)
    rims_in("two_01", (0, 1))

    def outer(h0):
        d = dot(s2, t2, ((0, 1), (1, 2)), h0)
        finish(d[:, EARLY], 0, h0)
        finish(d[:, LATE] + pair[rows_of(h0), LATE], 1, h0)
    blocks(outer)

    def one(h0):
        finish(acc[rows_of(h0), EARLY] + dot(s2, t2, ((1, 0),), h0, lanes=EARLY), 2, h0)
    blocks(one)

    wait_rims("two_cut")
    for i in range(3):
        face2_copy(i).wait_recv()
    def face_shift(k, _):
        a = s2[T, pl.ds(1 + R * k, R), :, MID].astype(F32)
        shifted(s2, T, 1 + R * k, R, a)
        return 0
    lax.fori_loop(0, H // R, face_shift, 0)
    rim_rows(s2, cr2, T)
    insert(s2, cr2, T)

    def last(h0):
        finish(acc[rows_of(h0), LATE] + dot(s2, t2, ((T, 3),), h0, lanes=LATE), 3, h0)
    blocks(last)

    for group in groups:
        wait_lines(send.at[names.index(group)], lines(group))
    for i in range(3):
        face_copy(i).wait_send()
        face2_copy(i).wait_send()


def place(x_ref, o_ref, sem):
    copies = [pltpu.make_async_copy(x_ref.at[g], o_ref.at[g], sem.at[g]) for g in range(T)]
    for c in copies:
        c.start()
    for c in copies:
        c.wait()


def body(features, kernel_one, kernel_two):
    out = pl.pallas_call(
        kernel,
        out_shape=jax.ShapeDtypeStruct((T, H, W, C), BF16),
        in_specs=[pl.BlockSpec(memory_space=pltpu.HBM)] * 3,
        out_specs=pl.BlockSpec(memory_space=pltpu.VMEM),
        scratch_shapes=[
            pltpu.VMEM((T, H, W, C), BF16),
            pltpu.VMEM((H, W, C), BF16),
            pltpu.VMEM((2, T + 1, W, C), BF16),
            pltpu.VMEM((T + 1, H + 2, W, 3 * C), BF16),
            pltpu.VMEM((T + 1, H + 2, W, 3 * C), BF16),
            pltpu.VMEM((4, 9, C, 2 * C), BF16),
            pltpu.VMEM((4, 9, C, 2 * C), BF16),
            pltpu.VMEM((H * W, 2 * C), F32),
            pltpu.VMEM((H * W, 2 * C), F32),
            pltpu.VMEM((2, T, H, 1, C), F32),
            pltpu.VMEM((2, T + 1, H + 2, 1, C), F32),
            pltpu.VMEM((2, T, H, 1, C), F32),
            pltpu.VMEM((2, T + 1, H + 2, 1, C), F32),
            pltpu.VMEM((R, W + 16, C), F32),
            pltpu.VMEM((288, 1, C), F32),
            pltpu.SemaphoreType.DMA((14,)),
            pltpu.SemaphoreType.DMA((14,)),
            pltpu.SemaphoreType.DMA((T + 12,)),
        ],
        compiler_params=pltpu.CompilerParams(
            collective_id=0, has_side_effects=True, vmem_limit_bytes=26 << 20),
        name="resblock",
    )(*(pltpu.with_memory_space_constraint(a, pltpu.HBM) for a in (
        features, kernel_one.reshape(3, 9, C, C), kernel_two.reshape(3, 9, C, C))))
    return pl.pallas_call(
        place, out_shape=jax.ShapeDtypeStruct((T, H, W, C), BF16),
        in_specs=[pl.BlockSpec(memory_space=pl.ANY)], out_specs=pl.BlockSpec(memory_space=pl.ANY),
        scratch_shapes=[pltpu.SemaphoreType.DMA((T,))],
        compiler_params=pltpu.CompilerParams(vmem_limit_bytes=1 << 20), name="place")(out)


def solution(mesh):
    return jax.shard_map(
        body,
        mesh=mesh,
        in_specs=(P("ta", "ha", "wa", None), P(), P()),
        out_specs=P("ta", "ha", "wa", None),
        check_vma=False,
    )
```
